512 devices in a mesh: pos: 64 (over z, y_hi, core), off: 8 (over x, y_lo).
Axes of the slice: x: 4, y: 8 (y_hi: 4, y_lo: 2; y = y_hi * 2 + y_lo), z: 8, core: 2. Of those that a mesh axis runs over, the one named last changes fastest.
Arguments:
- band_in: bfloat16 [32, 1024, 1024], P(None, 'pos', 'off'), may hold values from -6 to 6
- conv_weight: bfloat16 [2, 9, 32, 32], replicated, may hold values from -0.375 to 0.375
- mix_weight: bfloat16 [2, 32, 32], replicated, may hold values from -1 to 1
- norm_gain: float32 [2, 32], replicated, may hold values from 0.1 to 1.9
- norm_bias: float32 [2, 32], replicated, may hold values from -3 to 3
- cotangent: bfloat16 [32, 1024, 1024], P(None, 'pos', 'off'), may hold values from -6 to 6
Outputs:
- grad_band: bfloat16 [32, 1024, 1024], P(None, 'pos', 'off')
- grad_conv: float32 [2, 9, 32, 32], replicated
- grad_mix: float32 [2, 32, 32], replicated
- grad_gain: float32 [2, 32], replicated
- grad_bias: float32 [2, 32], replicated
The draws below stay inside these ranges and needn't reach their ends.
All inputs are finite; a program needn't handle non-finite values.
Results may differ from the reference program's by a relative error of at most 0.0095.
Values may be sent and summed in bfloat16 or wider, within the bound.
No kernel may reach another device: no remote copies, remote signals or barrier semaphores. Data moves between devices by JAX's collectives and lax.ppermute only.
A program may use at most 64 MiB of HBM per device.

```python
import math
import jax
import jax.numpy as jnp
from jax import lax

CH = 32
BAND = 1024
FIRST_DILATION = 2
SECOND_DILATION = 4
NPOS = 1024


def levels(rng, dims, pieces, smallest, largest):
    loudness, own = 1.0, jax.random.fold_in(rng, 6)
    for axis_at, parts in pieces:
        steps = jnp.exp(jax.random.uniform(jax.random.fold_in(own, axis_at), (parts,), jnp.float32, smallest / len(pieces), largest / len(pieces)))
        loudness = loudness * jnp.repeat(steps, dims[axis_at] // parts).reshape([-1 if axis == axis_at else 1 for axis in range(len(dims))])
    return loudness


def gaussian(rng, shape, scale, reach, split=(), held_as=jnp.bfloat16):
    factor_of = levels(rng, shape, split, -0.22, 0.18) if split else 1.0
    values = jax.random.normal(rng, shape, jnp.float32) * scale * factor_of
    return jnp.minimum(jnp.maximum(values, -reach), reach).astype(held_as)


def setup_inputs(seed: int = 0) -> dict:
    seeds = jax.random.split(jax.random.key(seed), 7)
    return {
        "band_in": gaussian(seeds[0], (CH, NPOS, BAND), 1.0, 6.0, ((1, 64), (2, 8))),
        "conv_weight": gaussian(seeds[1], (2, 9, CH, CH), (9 * CH) ** -0.5, 0.375),
        "mix_weight": gaussian(seeds[2], (2, CH, CH), CH ** -0.5, 1.0),
        "norm_gain": jnp.clip(1.0 + 0.18 * jax.random.normal(seeds[3], (2, CH), jnp.float32), 0.1, 1.9),
        "norm_bias": gaussian(seeds[4], (2, CH), 0.5, 3.0, (), jnp.float32),
        "cotangent": gaussian(seeds[5], (CH, NPOS, BAND), 1.0, 6.0, ((1, 64), (2, 8))),
    }


def tap_list(dilation):
    offsets = []
    for along_row in (-dilation, 0, dilation):
        for along_col in (-dilation, 0, dilation):
            offsets.append(((along_row + along_col) // 2, along_col - along_row))
    return offsets

def padded(source, dilation):
    return jnp.pad(source, ((0, 0), (dilation, dilation), (2 * dilation, 2 * dilation)))

def window(extended, dilation, row_count, column_count, row_shift, col_shift):
    row_start = dilation + row_shift
    column_start = 2 * dilation + col_shift
    return lax.slice(extended, (0, row_start, column_start), (extended.shape[0], row_start + row_count, column_start + column_count))

def smooth(values):
    return values * jax.nn.sigmoid(1.702 * values)

def smooth_slope(values):
    logistic = jax.nn.sigmoid(1.702 * values)
    return logistic + 1.702 * values * logistic * (1.0 - logistic)

def mirror(source):
    flipped = source[:, :, ::-1]
    return jnp.concatenate([jnp.zeros_like(source[:, :, :1]), flipped[:, :, :-1]], axis=2)

def apply_mix(matrix, source):
    return jnp.einsum('oi,iqc->oqc', matrix.astype(jnp.float32), source.astype(jnp.float32))

def apply_back(matrix, source):
    return jnp.einsum('oi,oqc->iqc', matrix.astype(jnp.float32), source.astype(jnp.float32))

def contract(left, right):
    return jnp.einsum('oqc,iqc->oi', left.astype(jnp.float32), right.astype(jnp.float32))

def reference(band_in, conv_weight, mix_weight, norm_gain, norm_bias, cotangent):
    row_count = band_in.shape[1]
    column_count = band_in.shape[2]
    grad_scale = 1.0 / math.sqrt(row_count * column_count)
    dilation_list = (FIRST_DILATION, SECOND_DILATION)
    current = band_in
    stored = []
    for section_index in range(2):
        dilation = dilation_list[section_index]
        activated = smooth(current.astype(jnp.float32)).astype(jnp.bfloat16)
        extended = padded(activated, dilation)
        pre_conv = jnp.zeros(current.shape, jnp.float32)
        for tap_index, shifts in enumerate(tap_list(dilation)):
            pre_conv = pre_conv + apply_mix(conv_weight[section_index, tap_index], window(extended, dilation, row_count, column_count, shifts[0], shifts[1]))
        gain_col = norm_gain[section_index][:, None, None]
        bias_col = norm_bias[section_index][:, None, None]
        hidden = smooth(gain_col * pre_conv + bias_col).astype(jnp.bfloat16)
        summed = (current.astype(jnp.float32) + apply_mix(mix_weight[section_index], hidden)).astype(jnp.bfloat16)
        stored.append((current, extended, pre_conv, hidden))
        current = ((summed.astype(jnp.float32) + mirror(summed).astype(jnp.float32)) * 0.5).astype(jnp.bfloat16)
    gradient = cotangent
    conv_parts = [None, None]
    mix_parts = [None, None]
    gain_pieces = [None, None]
    bias_parts = [None, None]
    for section_index in (1, 0):
        dilation = dilation_list[section_index]
        source, extended, pre_conv, hidden = stored[section_index]
        gain_col = norm_gain[section_index][:, None, None]
        bias_col = norm_bias[section_index][:, None, None]
        grad_sum = ((gradient.astype(jnp.float32) + mirror(gradient).astype(jnp.float32)) * 0.5).astype(jnp.bfloat16)
        mix_parts[section_index] = contract(grad_sum, hidden) * grad_scale
        grad_hidden = apply_back(mix_weight[section_index], grad_sum)
        grad_pre = grad_hidden * smooth_slope(gain_col * pre_conv + bias_col)
        gain_pieces[section_index] = lax.optimization_barrier(jnp.sum(grad_pre * pre_conv, axis=(1, 2))) * grad_scale
        bias_parts[section_index] = lax.optimization_barrier(jnp.sum(grad_pre, axis=(1, 2))) * grad_scale
        grad_conv_in = (grad_pre * gain_col).astype(jnp.bfloat16)
        grad_ext = padded(grad_conv_in, dilation)
        grad_act = jnp.zeros(source.shape, jnp.float32)
        tap_contributions = []
        for tap_index, shifts in enumerate(tap_list(dilation)):
            tap_contributions.append(contract(grad_conv_in, window(extended, dilation, row_count, column_count, shifts[0], shifts[1])) * grad_scale)
            grad_act = grad_act + apply_back(conv_weight[section_index, tap_index], window(grad_ext, dilation, row_count, column_count, -shifts[0], -shifts[1]))
        conv_parts[section_index] = jnp.stack(tap_contributions)
        gradient = (grad_sum.astype(jnp.float32) + grad_act * smooth_slope(source.astype(jnp.float32))).astype(jnp.bfloat16)
    return (gradient, jnp.stack(conv_parts), jnp.stack(mix_parts), jnp.stack(gain_pieces), jnp.stack(bias_parts))
```

```python
import math

import jax
import jax.numpy as jnp
from jax import lax
from jax.sharding import PartitionSpec as P

FIRST_DILATION = 2
SECOND_DILATION = 4


def with_halo(shard, sides, width):
    for axis, dim in sides:
        devices, length = (lax.axis_size(axis), shard.shape[dim])
        up = [(i, (i + 1) % devices) for i in range(devices - 1)]
        down = [(j, i) for i, j in up]
        last = lax.slice_in_dim(shard, length - width, length, axis=dim)
        first = lax.slice_in_dim(shard, 0, width, axis=dim)
        before = lax.ppermute(last, axis, up)
        after = lax.ppermute(first, axis, down)
        shard = jnp.concatenate([before, shard, after], axis=dim)
    return shard


def summed_over_mesh(flat):
    rows, columns = (lax.axis_size("pos"), lax.axis_size("off"))
    pad = -flat.shape[0] % (rows * 128)
    parts = jnp.pad(flat, (0, pad)).reshape(rows, -1)
    part = jnp.sum(lax.all_to_all(parts, "pos", 0, 0, tiled=True), axis=0)
    copies = jnp.broadcast_to(part[None], (columns,) + part.shape)
    part = jnp.sum(lax.all_to_all(copies, "off", 0, 0, tiled=True), axis=0)
    copies = jnp.broadcast_to(part[None], (rows,) + part.shape)
    return lax.all_to_all(copies, "pos", 0, 0, tiled=True).reshape(-1)[: flat.shape[0]]


def tap_list(dilation):
    offsets = []
    for along_row in (-dilation, 0, dilation):
        for along_col in (-dilation, 0, dilation):
            offsets.append(((along_row + along_col) // 2, along_col - along_row))
    return offsets


def window(extended, dilation, row_count, column_count, row_shift, col_shift):
    row_start = dilation + row_shift
    column_start = 2 * dilation + col_shift
    return lax.slice(
        extended,
        (0, row_start, column_start),
        (extended.shape[0], row_start + row_count, column_start + column_count),
    )


def smooth(values):
    return values * jax.nn.sigmoid(1.702 * values)


def smooth_slope(values):
    logistic = jax.nn.sigmoid(1.702 * values)
    return logistic + 1.702 * values * logistic * (1.0 - logistic)


def extend(source, dilation):
    tall_ext = with_halo(source, (("pos", 1),), dilation)
    return with_halo(tall_ext, (("off", 2),), 2 * dilation)


def reflect(source):
    devices = lax.axis_size("off")
    opposite = lax.ppermute(source, "off", [(i, devices - 1 - i) for i in range(devices)])
    edge_col = lax.ppermute(source[:, :, :1], "off", [(devices - i, i) for i in range(1, devices)])
    return jnp.concatenate([edge_col, opposite[:, :, :0:-1]], axis=2)


def local(band_in, conv_weight, mix_weight, norm_gain, norm_bias, cotangent):
    row_count = band_in.shape[1]
    column_count = band_in.shape[2]
    grad_scale = 1.0 / math.sqrt(
        row_count * lax.axis_size("pos") * column_count * lax.axis_size("off")
    )
    dilation_list = (FIRST_DILATION, SECOND_DILATION)
    current = band_in
    stored = []
    for section_index in range(2):
        dilation = dilation_list[section_index]
        activated = smooth(current.astype(jnp.float32)).astype(jnp.bfloat16)
        extended = extend(activated, dilation)
        pre_conv = jnp.zeros(current.shape, jnp.float32)
        for tap_index, shifts in enumerate(tap_list(dilation)):
            pre_conv = pre_conv + jnp.einsum(
                "oi,iqc->oqc",
                conv_weight[section_index, tap_index],
                window(extended, dilation, row_count, column_count, shifts[0], shifts[1]),
                preferred_element_type=jnp.float32,
            )
        gain_col = norm_gain[section_index][:, None, None]
        bias_col = norm_bias[section_index][:, None, None]
        hidden = smooth(gain_col * pre_conv + bias_col).astype(jnp.bfloat16)
        mixed = jnp.einsum(
            "oi,iqc->oqc", mix_weight[section_index], hidden, preferred_element_type=jnp.float32
        )
        summed = (current.astype(jnp.float32) + mixed).astype(jnp.bfloat16)
        stored.append((current, extended, pre_conv, hidden))
        current = ((summed.astype(jnp.float32) + reflect(summed).astype(jnp.float32)) * 0.5).astype(
            jnp.bfloat16
        )
    gradient = cotangent
    grad_parts = [None, None]
    for section_index in (1, 0):
        dilation = dilation_list[section_index]
        source, extended, pre_conv, hidden = stored[section_index]
        gain_col = norm_gain[section_index][:, None, None]
        bias_col = norm_bias[section_index][:, None, None]
        grad_sum = (
            (gradient.astype(jnp.float32) + reflect(gradient).astype(jnp.float32)) * 0.5
        ).astype(jnp.bfloat16)
        mix_term = jnp.einsum("oqc,iqc->oi", grad_sum, hidden, preferred_element_type=jnp.float32)
        grad_hidden = jnp.einsum(
            "oi,oqc->iqc", mix_weight[section_index], grad_sum, preferred_element_type=jnp.float32
        )
        grad_pre = grad_hidden * smooth_slope(gain_col * pre_conv + bias_col)
        gain_term = jnp.sum(grad_pre * pre_conv, axis=(1, 2))
        bias_term = jnp.sum(grad_pre, axis=(1, 2))
        grad_conv_in = (grad_pre * gain_col).astype(jnp.bfloat16)
        grad_ext = extend(grad_conv_in, dilation)
        grad_act = jnp.zeros(source.shape, jnp.float32)
        tap_contributions = []
        for tap_index, shifts in enumerate(tap_list(dilation)):
            tap_contributions.append(
                jnp.einsum(
                    "oqc,iqc->oi",
                    grad_conv_in,
                    window(extended, dilation, row_count, column_count, shifts[0], shifts[1]),
                    preferred_element_type=jnp.float32,
                )
            )
            grad_act = grad_act + jnp.einsum(
                "oi,oqc->iqc",
                conv_weight[section_index, tap_index],
                window(grad_ext, dilation, row_count, column_count, -shifts[0], -shifts[1]),
                preferred_element_type=jnp.float32,
            )
        gradient = (
            grad_sum.astype(jnp.float32) + grad_act * smooth_slope(source.astype(jnp.float32))
        ).astype(jnp.bfloat16)
        tap_stack = jnp.stack(tap_contributions)
        grad_parts[section_index] = (tap_stack, mix_term, gain_term, bias_term)
    conv_total = jnp.stack([grad_parts[0][0], grad_parts[1][0]])
    mix_total = jnp.stack([grad_parts[0][1], grad_parts[1][1]])
    gain_total = jnp.stack([grad_parts[0][2], grad_parts[1][2]])
    bias_total = jnp.stack([grad_parts[0][3], grad_parts[1][3]])
    totals = (conv_total, mix_total, gain_total, bias_total)
    flat = summed_over_mesh(jnp.concatenate([total.reshape(-1) for total in totals]))
    starts = [0]
    for total in totals:
        starts.append(starts[-1] + total.size)
    conv_total, mix_total, gain_total, bias_total = (
        flat[start : start + total.size].reshape(total.shape)
        for start, total in zip(starts, totals)
    )
    return (
        gradient,
        conv_total * grad_scale,
        mix_total * grad_scale,
        gain_total * grad_scale,
        bias_total * grad_scale,
    )


def solution(mesh):
    placed = (P(None, "pos", "off"), P(), P(), P(), P(), P(None, "pos", "off"))
    return jax.shard_map(
        local,
        mesh=mesh,
        in_specs=placed,
        out_specs=(P(None, "pos", "off"), P(), P(), P(), P()),
        check_vma=False,
    )
```

```python
import math

import jax
import jax.numpy as jnp
from jax import lax
from jax.experimental import pallas as pl
from jax.experimental.pallas import tpu as pltpu
from jax.sharding import PartitionSpec as P

FIRST_DILATION = 2
SECOND_DILATION = 4
CH = 32
TAPS = 9
WIDE_ROWS = 2 * (FIRST_DILATION + SECOND_DILATION)
NARROW_ROWS = FIRST_DILATION + SECOND_DILATION
WIDE_COLS = 32
NARROW_COLS = 16
LANES = 256
GRAD_COLS = 384

SLOPE = 1.702


def tap_list(dilation):
    offsets = []
    for along_row in (-dilation, 0, dilation):
        for along_col in (-dilation, 0, dilation):
            offsets.append(((along_row + along_col) // 2, along_col - along_row))
    return offsets


def logistic(values):
    return 0.5 + 0.5 * jnp.tanh((0.5 * SLOPE) * values)


def smooth(values):
    return values * logistic(values)


def slope_of(values, gate):
    return gate + SLOPE * values * gate * (1.0 - gate)


def twin(halves):
    return jnp.concatenate(halves, axis=0)


def body(
    place,
    wide,
    narrow,
    conv,
    conv_back,
    conv_back_own,
    mix,
    mix_back,
    gain,
    bias,
    out,
    grads,
    act0,
    act1,
    back1,
    back0,
    mid,
    pre0,
    hid0,
    gsum0,
    hid1,
    gsum1,
    sums,
):
    rows = out.shape[0]
    tile = out.shape[2]
    total_rows, total_cols = (place[2], place[3])
    first_row, first_col = (place[0], place[1])
    lane = lax.broadcasted_iota(jnp.int32, (1, LANES), 1)
    column = first_col + jnp.where(lane < LANES - 64, lane, lane - LANES)
    own_ok = jnp.where((column >= 0) & (column < total_cols), 1.0, 0.0)
    mir_ok = jnp.where((column > 0) & (column <= total_cols), 1.0, 0.0)

    def row_ok(local_row):
        row = first_row + local_row
        return jnp.where((row >= 0) & (row < total_rows), 1.0, 0.0)

    def spread(target, index, values, dilation):
        for step in range(-2, 3):
            moved = values
            if step:
                moved = pltpu.roll(values, (-step * dilation) % LANES, 1)
            target[step + 2, index] = moved.astype(jnp.bfloat16)

    def stacked(source, index, dilation, sign, part=slice(None), lanes=slice(None)):
        pieces = []
        for row_shift, col_shift in tap_list(dilation):
            pieces.append(
                source[sign * col_shift // dilation + 2, index + sign * row_shift, part, lanes]
            )
        return jnp.concatenate(pieces, axis=0)

    def dot(left, right):
        return jnp.dot(left, right, preferred_element_type=jnp.float32)

    def own_dot(left, right):
        return lax.dot_general(
            left, right, (((1,), (1,)), ((), ())), preferred_element_type=jnp.float32
        )

    gains = [gain[s] for s in range(2)]
    biases = [bias[s] for s in range(2)]
    gains2 = [twin([g, g]) for g in gains]
    biases2 = [twin([b, b]) for b in biases]
    sums[...] = jnp.zeros_like(sums)

    def first_act(q, carry):
        values = wide[q].astype(jnp.float32)
        values = twin([values[:CH], pltpu.roll(values[CH:], 1, 1)])
        spread(act0, q, smooth(values), FIRST_DILATION)
        return carry

    lax.fori_loop(0, rows + 2 * WIDE_ROWS, first_act, 0)

    def first_block(n, carry):
        q = n + FIRST_DILATION
        pre = dot(conv[0], stacked(act0, q, FIRST_DILATION, 1))
        shifted = gains2[0] * pre + biases2[0]
        hidden = smooth(shifted).astype(jnp.bfloat16)
        mixed = dot(mix[0], hidden)
        values = wide[q].astype(jnp.float32)
        values = twin([values[:CH], pltpu.roll(values[CH:], 1, 1)])
        summed = (values + mixed).astype(jnp.bfloat16).astype(jnp.float32)
        both = (summed[:CH] * own_ok + summed[CH:] * mir_ok) * (0.5 * row_ok(q - WIDE_ROWS))
        both = both.astype(jnp.bfloat16)
        mid[n] = both
        act = smooth(both.astype(jnp.float32))
        spread(act1, n, twin([act * own_ok, act * mir_ok]), SECOND_DILATION)
        inner = q - (WIDE_ROWS - FIRST_DILATION)

        @pl.when((inner >= 0) & (inner < rows + 2 * FIRST_DILATION))
        def _():
            pre0[inner] = pre[:CH]
            hid0[inner] = hidden[:CH]

        return carry

    lax.fori_loop(0, rows + 2 * (WIDE_ROWS - FIRST_DILATION), first_block, 0)

    def second_block(n, carry):
        q = n + SECOND_DILATION
        pre = dot(conv[1], stacked(act1, q, SECOND_DILATION, 1))
        shifted = gains2[1] * pre + biases2[1]
        gate = logistic(shifted)
        cot = narrow[n].astype(jnp.float32)
        total = ((cot[:CH] + pltpu.roll(cot[CH:], 1, 1)) * 0.5).astype(jnp.bfloat16)
        grad = dot(mix_back[1], total)
        grad_pre = twin([grad * own_ok, grad * mir_ok]) * slope_of(shifted, gate)
        grad_conv = grad_pre * gains2[1]
        spread(back1, n, grad_conv, SECOND_DILATION)
        gsum1[n] = total
        inner = n - NARROW_ROWS

        @pl.when((inner >= 0) & (inner < rows))
        def _():
            hid1[inner] = (shifted * gate)[:CH, :tile].astype(jnp.bfloat16)
            own = grad_pre[:CH, :tile]
            sums[2] += own * pre[:CH, :tile]
            sums[3] += own

        return carry

    lax.fori_loop(0, rows + 2 * NARROW_ROWS, second_block, 0)

    def between(n, carry):
        back = dot(conv_back[1], stacked(back1, n + SECOND_DILATION, SECOND_DILATION, -1))
        values = mid[n + NARROW_ROWS + FIRST_DILATION].astype(jnp.float32)
        slope = slope_of(values, logistic(values))
        total = gsum1[n + SECOND_DILATION].astype(jnp.float32)
        grad_in = twin([total, total]) + twin([slope, slope]) * back
        grad_in = grad_in.astype(jnp.bfloat16).astype(jnp.float32)
        both = (grad_in[:CH] * own_ok + grad_in[CH:] * mir_ok) * 0.5
        both = (both * (own_ok * row_ok(n - FIRST_DILATION))).astype(jnp.bfloat16)
        grad = dot(mix_back[0], both)
        pre = pre0[n]
        shifted = gains[0] * pre + biases[0]
        grad_pre = grad * slope_of(shifted, logistic(shifted))
        spread(back0, n, grad_pre * gains[0], FIRST_DILATION)
        gsum0[n] = both

        @pl.when((n >= FIRST_DILATION) & (n < rows + FIRST_DILATION))
        def _():
            own = grad_pre[:, :tile]
            sums[0] += own * pre[:, :tile]
            sums[1] += own

        return carry

    lax.fori_loop(0, rows + 2 * FIRST_DILATION, between, 0)

    near = slice(0, tile)
    own = slice(0, CH)

    def finish(m, carry):
        conv0, conv1, mix0, mix1 = carry

        def pair(load):
            return jnp.concatenate([load(2 * m), load(2 * m + 1)], axis=1)

        back = dot(
            conv_back_own[...],
            pair(lambda n: stacked(back0, n + FIRST_DILATION, FIRST_DILATION, -1, own, near)),
        )
        values = pair(lambda n: wide[n + WIDE_ROWS, own, near]).astype(jnp.float32)
        total0 = pair(lambda n: gsum0[n + FIRST_DILATION, :, near])
        result = total0.astype(jnp.float32) + slope_of(values, logistic(values)) * back
        result = result.astype(jnp.bfloat16)
        out[2 * m] = result[:, :tile]
        out[2 * m + 1] = result[:, tile:]
        grad0 = pair(lambda n: back0[2, n + FIRST_DILATION, :, near])
        grad1 = pair(lambda n: back1[2, n + NARROW_ROWS, own, near])
        stack0 = pair(lambda n: stacked(act0, n + WIDE_ROWS, FIRST_DILATION, 1, own, near))
        stack1 = pair(
            lambda n: stacked(
                act1, n + WIDE_ROWS - FIRST_DILATION, SECOND_DILATION, 1, own, near
            )
        )
        conv0 = conv0 + own_dot(grad0, stack0)
        conv1 = conv1 + own_dot(grad1, stack1)
        mix0 = mix0 + own_dot(total0, pair(lambda n: hid0[n + FIRST_DILATION, :, near]))
        total1 = pair(lambda n: gsum1[n + NARROW_ROWS, :, near])
        mix1 = mix1 + own_dot(total1, pair(lambda n: hid1[n]))
        return conv0, conv1, mix0, mix1

    wide_zero = jnp.zeros((CH, TAPS * CH), jnp.float32)
    small_zero = jnp.zeros((CH, CH), jnp.float32)
    conv0, conv1, mix0, mix1 = lax.fori_loop(
        0, rows // 2, finish, (wide_zero, wide_zero, small_zero, small_zero)
    )
    grads[...] = jnp.zeros_like(grads)
    edge = TAPS * CH
    for s, (conv_s, mix_s) in enumerate(((conv0, mix0), (conv1, mix1))):
        part = slice(s * CH, (s + 1) * CH)
        grads[part, 0:edge] = conv_s
        grads[part, edge : edge + CH] = mix_s
        grads[part, edge + CH : edge + CH + 1] = jnp.sum(sums[2 * s], axis=1, keepdims=True)
        grads[part, edge + CH + 1 : edge + CH + 2] = jnp.sum(
            sums[2 * s + 1], axis=1, keepdims=True
        )


def swap_mesh_tap(weights):
    return weights.reshape((3, 3) + weights.shape[1:]).swapaxes(0, 1).reshape(weights.shape)


def two_sided(weights):
    other = swap_mesh_tap(weights)
    zero = jnp.zeros_like(weights)
    top = jnp.concatenate([weights, zero], axis=2)
    low = jnp.concatenate([zero, other], axis=2)
    both = jnp.concatenate([top, low], axis=1)
    return both.transpose(1, 0, 2).reshape(2 * CH, TAPS * 2 * CH)


def on_tile(wide, narrow, place, conv_weight, mix_weight, norm_gain, norm_bias, rows, tile):
    back = conv_weight.swapaxes(2, 3)
    mix_back = mix_weight.swapaxes(1, 2)
    zero = jnp.zeros_like(mix_weight)
    mix_two = jnp.concatenate(
        [
            jnp.concatenate([mix_weight, zero], axis=2),
            jnp.concatenate([zero, mix_weight], axis=2),
        ],
        axis=1,
    )
    operands = (
        place,
        wide,
        narrow,
        jnp.stack([two_sided(conv_weight[s]) for s in range(2)]),
        jnp.stack([two_sided(back[s]) for s in range(2)]),
        back[0].transpose(1, 0, 2).reshape(CH, TAPS * CH),
        mix_two,
        mix_back,
        norm_gain[:, :, None],
        norm_bias[:, :, None],
    )
    bf16, f32 = (jnp.bfloat16, jnp.float32)
    wide_rows = rows + 2 * WIDE_ROWS
    mid_rows = wide_rows - 2 * FIRST_DILATION
    narrow_rows = rows + 2 * NARROW_ROWS
    inner_rows = rows + 2 * FIRST_DILATION
    vmem = pl.BlockSpec(memory_space=pltpu.VMEM)
    return pl.pallas_call(
        body,
        out_shape=(
            jax.ShapeDtypeStruct((rows, CH, tile), bf16),
            jax.ShapeDtypeStruct((2 * CH, GRAD_COLS), f32),
        ),
        in_specs=[pl.BlockSpec(memory_space=pltpu.SMEM)] + [vmem] * (len(operands) - 1),
        out_specs=(vmem, vmem),
        scratch_shapes=[
            pltpu.VMEM((5, wide_rows, 2 * CH, LANES), bf16),
            pltpu.VMEM((5, mid_rows, 2 * CH, LANES), bf16),
            pltpu.VMEM((5, narrow_rows, 2 * CH, LANES), bf16),
            pltpu.VMEM((5, inner_rows, CH, LANES), bf16),
            pltpu.VMEM((mid_rows, CH, LANES), bf16),
            pltpu.VMEM((inner_rows, CH, LANES), f32),
            pltpu.VMEM((inner_rows, CH, LANES), bf16),
            pltpu.VMEM((inner_rows, CH, LANES), bf16),
            pltpu.VMEM((rows, CH, tile), bf16),
            pltpu.VMEM((narrow_rows, CH, LANES), bf16),
            pltpu.VMEM((4, CH, tile), f32),
        ],
        compiler_params=pltpu.CompilerParams(vmem_limit_bytes=48 * 1024 * 1024),
        name="blocks_backward",
    )(*operands)


def gather_sides(axis, down, up):
    devices = lax.axis_size(axis)
    before = lax.ppermute(down, axis, [(i, i + 1) for i in range(devices - 1)])
    after = lax.ppermute(up, axis, [(i + 1, i) for i in range(devices - 1)])
    return before, after


def packed(wide, narrow, last):
    rows, narrow_rows = (wide.shape[0], narrow.shape[0])
    cut = slice(-WIDE_COLS, None) if last else slice(0, WIDE_COLS)
    wide = wide[:, :, cut]
    per = 128 // WIDE_COLS
    wide = jnp.concatenate(jnp.split(wide, per, axis=0), axis=2)
    cut = slice(-NARROW_COLS, None) if last else slice(0, NARROW_COLS)
    narrow = narrow[:, :, cut]
    per = 128 // NARROW_COLS
    fill = -narrow_rows % per
    narrow = jnp.concatenate([narrow, narrow[:fill]], axis=0)
    narrow = jnp.concatenate(jnp.split(narrow, per, axis=0), axis=2)
    return jnp.concatenate([wide, narrow], axis=0)


def unpacked(message, wide_rows, narrow_rows):
    per = 128 // WIDE_COLS
    count = wide_rows // per
    wide = jnp.concatenate(jnp.split(message[:count], per, axis=2), axis=0)
    per = 128 // NARROW_COLS
    narrow = jnp.concatenate(jnp.split(message[count:], per, axis=2), axis=0)
    return wide, narrow[:narrow_rows]


def with_surroundings(band, cotangent):
    devices = lax.axis_size("off")
    mine = jnp.concatenate([band, cotangent], axis=1)
    other = lax.ppermute(mine[:, :, ::-1], "off", [(i, devices - 1 - i) for i in range(devices)])
    wide = jnp.concatenate([band, other[:, :CH]], axis=1)
    narrow = jnp.concatenate([cotangent, other[:, CH:]], axis=1)
    before, after = gather_sides(
        "pos",
        jnp.concatenate([wide[-WIDE_ROWS:], narrow[-NARROW_ROWS:]], axis=0),
        jnp.concatenate([wide[:WIDE_ROWS], narrow[:NARROW_ROWS]], axis=0),
    )
    wide = jnp.concatenate([before[:WIDE_ROWS], wide, after[:WIDE_ROWS]], axis=0)
    narrow = jnp.concatenate([before[WIDE_ROWS:], narrow, after[WIDE_ROWS:]], axis=0)
    before, after = gather_sides(
        "off", packed(wide, narrow, True), packed(wide, narrow, False)
    )
    before = unpacked(before, wide.shape[0], narrow.shape[0])
    after = unpacked(after, wide.shape[0], narrow.shape[0])
    full = []
    for tile, low, high in zip((wide, narrow), before, after):
        gap = LANES - tile.shape[2] - low.shape[2] - high.shape[2]
        zero = jnp.zeros(tile.shape[:2] + (gap,), tile.dtype)
        full.append(jnp.concatenate([tile, high, zero, low], axis=2))
    return full


def summed_over_mesh(parts):
    rows, columns = (lax.axis_size("pos"), lax.axis_size("off"))
    whole = parts.shape
    parts = parts.reshape(rows, -1)
    part = jnp.sum(lax.all_to_all(parts, "pos", 0, 0, tiled=True), axis=0)
    copies = jnp.broadcast_to(part[None], (columns,) + part.shape)
    part = jnp.sum(lax.all_to_all(copies, "off", 0, 0, tiled=True), axis=0)
    copies = jnp.broadcast_to(part[None], (rows,) + part.shape)
    return lax.all_to_all(copies, "pos", 0, 0, tiled=True).reshape(whole)


def local(band_in, conv_weight, mix_weight, norm_gain, norm_bias, cotangent):
    rows, tile = band_in.shape[1:]
    total_rows = rows * lax.axis_size("pos")
    total_cols = tile * lax.axis_size("off")
    grad_scale = 1.0 / math.sqrt(total_rows * total_cols)
    place = jnp.stack(
        [
            lax.axis_index("pos") * rows,
            lax.axis_index("off") * tile,
            jnp.int32(total_rows),
            jnp.int32(total_cols),
        ]
    )
    wide, narrow = with_surroundings(band_in.swapaxes(0, 1), cotangent.swapaxes(0, 1))
    gradient, grads = on_tile(
        wide, narrow, place, conv_weight, mix_weight, norm_gain, norm_bias, rows, tile
    )
    edge = TAPS * CH
    totals = summed_over_mesh(grads).reshape(2, CH, GRAD_COLS) * grad_scale
    conv_total = totals[:, :, :edge].reshape(2, CH, TAPS, CH).swapaxes(1, 2)
    return (
        gradient.swapaxes(0, 1),
        conv_total,
        totals[:, :, edge : edge + CH],
        totals[:, :, edge + CH],
        totals[:, :, edge + CH + 1],
    )


def solution(mesh):
    placed = (P(None, "pos", "off"), P(), P(), P(), P(), P(None, "pos", "off"))
    return jax.shard_map(
        local,
        mesh=mesh,
        in_specs=placed,
        out_specs=(P(None, "pos", "off"), P(), P(), P(), P()),
        check_vma=False,
    )
```

```python
import math

import jax
import jax.numpy as jnp
from jax import lax
from jax.experimental import pallas as pl
from jax.experimental.pallas import tpu as pltpu
from jax.sharding import PartitionSpec as P

FIRST_DILATION = 2
SECOND_DILATION = 4
CH = 32
TAPS = 9
WIDE_ROWS = 2 * (FIRST_DILATION + SECOND_DILATION)
NARROW_ROWS = FIRST_DILATION + SECOND_DILATION
WIDE_COLS = 32
NARROW_COLS = 16
LANES = 256
GRAD_COLS = 384

SLOPE = 1.702


def tap_list(dilation):
    offsets = []
    for along_row in (-dilation, 0, dilation):
        for along_col in (-dilation, 0, dilation):
            offsets.append(((along_row + along_col) // 2, along_col - along_row))
    return offsets


def gated(values):
    half = 0.5 * values
    return half + half * jnp.tanh(SLOPE * half)


def twice_slope(halved, bent):
    return (1.0 + bent) * (1.0 + halved * (1.0 - bent))


def body(
    place,
    wide,
    narrow,
    conv,
    conv_back,
    conv_back_own,
    mix,
    mix_back,
    gain,
    bias,
    out,
    grads,
    act0,
    act1,
    back1,
    back0,
    mid,
    pre0,
    hid0,
    slope0,
    gsum0,
    hid1,
    gsum1,
    pre1,
    slope1,
    masks,
):
    rows = out.shape[0]
    tile = out.shape[2]
    bf16, f32 = (jnp.bfloat16, jnp.float32)
    first_row, first_col, total_rows, total_cols = [place[k] for k in range(4)]
    lane = lax.broadcasted_iota(jnp.int32, (CH, LANES), 1)
    column = first_col + jnp.where(lane < LANES - 64, lane, lane - LANES)
    masks[0] = jnp.where((column >= 0) & (column < total_cols), 1.0, 0.0).astype(bf16)
    masks[1] = jnp.where((column > 0) & (column <= total_cols), 1.0, 0.0).astype(bf16)

    def half_in_rows(local_row):
        row = first_row + local_row
        factor = jnp.where((row >= 0) & (row < total_rows), 0.5, 0.0)
        return jnp.broadcast_to(factor, (CH, LANES)).astype(bf16)

    def spread(target, index, values, dilation):
        stores = []
        for step in range(-2, 3):
            moved = values
            if step:
                moved = pltpu.roll(values, (-step * dilation) % LANES, 1)
            stores.append((target, (step + 2, index), moved))
        return stores

    def over_rows(count, at_once, stores_of):
        def step(m, carry):
            stores = [stores_of(at_once * m + k) for k in range(at_once)]
            for target, index, values in sum(stores, []):
                target[index] = values
            return carry

        lax.fori_loop(0, count // at_once, step, 0)

    def stacked(source, index, dilation, sign, part=slice(None), lanes=slice(None)):
        pieces = []
        for row_shift, col_shift in tap_list(dilation):
            pieces.append(
                source[sign * col_shift // dilation + 2, index + sign * row_shift, part, lanes]
            )
        return jnp.concatenate(pieces, axis=0)

    def dot(left, right):
        return jnp.dot(left, right, preferred_element_type=f32)

    def own_dot(left, right):
        return lax.dot_general(left, right, (((1,), (1,)), ((), ())), preferred_element_type=f32)

    def across(values, count=LANES):
        return jnp.concatenate([values] * (count // 128), axis=1)

    def both_halves(values):
        return jnp.concatenate([values, values], axis=0)

    def first_act(q):
        return spread(act0, q, gated(wide[q].astype(f32)).astype(bf16), FIRST_DILATION)

    over_rows(rows + 2 * WIDE_ROWS, 4, first_act)

    def first_block(n):
        q = n + FIRST_DILATION
        pre = dot(conv[0], stacked(act0, q, FIRST_DILATION, 1))
        hidden = gated(across(gain[0]) * pre + across(bias[0])).astype(bf16)
        summed = (wide[q].astype(f32) + dot(mix[0], hidden)).astype(bf16)
        other = pltpu.roll(summed[CH:], 1, 1)
        both = (summed[:CH] * masks[0] + other * masks[1]) * half_in_rows(q - WIDE_ROWS)
        act = gated(both.astype(f32)).astype(bf16)
        acts = jnp.concatenate([act * masks[0], act * masks[1]], axis=0)
        return spread(act1, n, acts, SECOND_DILATION) + [
            (mid, n, both),
            (pre0, n, pre[:CH]),
            (hid0, n, hidden[:CH, :tile]),
        ]

    over_rows(rows + 2 * (WIDE_ROWS - FIRST_DILATION), 4, first_block)

    def second_block(n):
        pre = dot(conv[1], stacked(act1, n + SECOND_DILATION, SECOND_DILATION, 1))
        halved = (0.5 * SLOPE) * (across(gain[1]) * pre + across(bias[1]))
        bent = jnp.tanh(halved)
        cot = narrow[n]
        total = (cot[:CH] + pltpu.roll(cot[CH:], 1, 1)) * jnp.asarray(0.5, bf16)
        sides = jnp.concatenate([total * masks[0], total * masks[1]], axis=0)
        grad_pre = dot(mix_back[1], sides) * twice_slope(halved, bent)
        hidden = (halved[:CH, :tile] * (1.0 / SLOPE)) * (1.0 + bent[:CH, :tile])
        grad_conv = (grad_pre * across(gain[1])).astype(bf16)
        return spread(back1, n, grad_conv, SECOND_DILATION) + [
            (gsum1, n, total),
            (pre1, n, pre[:CH, :tile]),
            (slope1, n, grad_pre[:CH, :tile]),
            (hid1, n, hidden.astype(bf16)),
        ]

    over_rows(rows + 2 * NARROW_ROWS, 4, second_block)

    def between(n):
        back = dot(conv_back[...], stacked(back1, n + SECOND_DILATION, SECOND_DILATION, -1))
        halved = (0.5 * SLOPE) * mid[n + NARROW_ROWS + FIRST_DILATION].astype(f32)
        slope = twice_slope(halved, jnp.tanh(halved))
        total = gsum1[n + SECOND_DILATION].astype(f32)
        grad_in = (both_halves(total) + both_halves(slope) * back).astype(bf16)
        both = grad_in[:CH] * masks[0] + grad_in[CH:] * masks[1]
        both = (both * masks[0]) * half_in_rows(n - FIRST_DILATION)
        pre = pre0[n + WIDE_ROWS - 2 * FIRST_DILATION]
        halved = (0.5 * SLOPE) * (across(gain[0, :CH]) * pre + across(bias[0, :CH]))
        grad_pre = dot(mix_back[0, :CH, :CH], both) * twice_slope(halved, jnp.tanh(halved))
        grad_conv = (grad_pre * across(gain[0, :CH])).astype(bf16)
        return spread(back0, n, grad_conv, FIRST_DILATION) + [
            (gsum0, n, both),
            (slope0, n, grad_pre[:, :tile]),
        ]

    over_rows(rows + 2 * FIRST_DILATION, 4, between)

    near = slice(0, tile)
    own = slice(0, CH)

    def finish(m, carry):
        conv0, conv1, mix0, mix1, gain0, bias0, gain1, bias1 = carry

        def pair(load):
            return jnp.concatenate([load(2 * m), load(2 * m + 1)], axis=1)

        back = dot(
            conv_back_own[...],
            pair(lambda n: stacked(back0, n + FIRST_DILATION, FIRST_DILATION, -1, own, near)),
        )
        values = pair(lambda n: wide[n + WIDE_ROWS, own, near]).astype(f32)
        halved = (0.5 * SLOPE) * values
        total0 = pair(lambda n: gsum0[n + FIRST_DILATION, :, near])
        result = total0.astype(f32) + twice_slope(halved, jnp.tanh(halved)) * back
        result = result.astype(bf16)
        out[2 * m] = result[:, :tile]
        out[2 * m + 1] = result[:, tile:]
        grad0 = pair(lambda n: back0[2, n + FIRST_DILATION, :, near])
        grad1 = pair(lambda n: back1[2, n + NARROW_ROWS, own, near])
        stack0 = pair(lambda n: stacked(act0, n + WIDE_ROWS, FIRST_DILATION, 1, own, near))
        stack1 = pair(
            lambda n: stacked(
                act1, n + WIDE_ROWS - FIRST_DILATION, SECOND_DILATION, 1, own, near
            )
        )
        conv0 = conv0 + own_dot(grad0, stack0)
        conv1 = conv1 + own_dot(grad1, stack1)
        mix0 = mix0 + own_dot(total0, pair(lambda n: hid0[n + WIDE_ROWS - FIRST_DILATION]))
        total1 = pair(lambda n: gsum1[n + NARROW_ROWS, :, near])
        mix1 = mix1 + own_dot(total1, pair(lambda n: hid1[n + NARROW_ROWS]))
        for n in (2 * m, 2 * m + 1):
            grad = slope0[n + FIRST_DILATION]
            bias0 = bias0 + grad
            gain0 = gain0 + grad * pre0[n + WIDE_ROWS - FIRST_DILATION, :, near]
            grad = slope1[n + NARROW_ROWS]
            bias1 = bias1 + grad
            gain1 = gain1 + grad * pre1[n + NARROW_ROWS]
        return conv0, conv1, mix0, mix1, gain0, bias0, gain1, bias1

    taps_zero = jnp.zeros((CH, TAPS * CH), f32)
    small_zero = jnp.zeros((CH, CH), f32)
    tile_zero = jnp.zeros((CH, tile), f32)
    start = (taps_zero,) * 2 + (small_zero,) * 2 + (tile_zero,) * 4
    conv0, conv1, mix0, mix1, gain0, bias0, gain1, bias1 = lax.fori_loop(
        0, rows // 2, finish, start, unroll=2
    )
    edge = TAPS * CH
    for s, parts in enumerate(((conv0, mix0, gain0, bias0), (conv1, mix1, gain1, bias1))):
        place_s = slice(s * CH, (s + 1) * CH)
        grads[place_s, 0:edge] = parts[0]
        sums = [jnp.sum(part, axis=1, keepdims=True) for part in parts[2:]]
        rest = jnp.zeros((CH, GRAD_COLS - edge - CH - 2), f32)
        grads[place_s, edge:] = jnp.concatenate([parts[1]] + sums + [rest], axis=1)


def swap_mesh_tap(weights):
    return weights.reshape((3, 3) + weights.shape[1:]).swapaxes(0, 1).reshape(weights.shape)


def two_sided(weights):
    other = swap_mesh_tap(weights)
    zero = jnp.zeros_like(weights)
    top = jnp.concatenate([weights, zero], axis=2)
    low = jnp.concatenate([zero, other], axis=2)
    both = jnp.concatenate([top, low], axis=1)
    return both.transpose(1, 0, 2).reshape(2 * CH, TAPS * 2 * CH)


def two_diagonal(weights):
    zero = jnp.zeros_like(weights)
    top = jnp.concatenate([weights, zero], axis=2)
    return jnp.concatenate([top, jnp.concatenate([zero, weights], axis=2)], axis=1)


def on_tile(wide, narrow, place, conv_weight, mix_weight, norm_gain, norm_bias, rows, tile):
    bf16, f32 = (jnp.bfloat16, jnp.float32)
    back = 0.5 * conv_weight.swapaxes(2, 3)

    def per_channel(values):
        return jnp.broadcast_to(jnp.tile(values, (1, 2))[:, :, None], (2, 2 * CH, 128))

    operands = (
        place,
        wide,
        narrow,
        jnp.stack([two_sided(conv_weight[s]) for s in range(2)]),
        two_sided(back[1]),
        back[0].transpose(1, 0, 2).reshape(CH, TAPS * CH),
        two_diagonal(mix_weight),
        two_diagonal(0.5 * mix_weight.swapaxes(1, 2)),
        per_channel(norm_gain),
        per_channel(norm_bias),
    )
    wide_rows = rows + 2 * WIDE_ROWS
    mid_rows = wide_rows - 2 * FIRST_DILATION
    narrow_rows = rows + 2 * NARROW_ROWS
    inner_rows = rows + 2 * FIRST_DILATION
    vmem = pl.BlockSpec(memory_space=pltpu.VMEM)
    return pl.pallas_call(
        body,
        out_shape=(
            jax.ShapeDtypeStruct((rows, CH, tile), bf16),
            jax.ShapeDtypeStruct((2 * CH, GRAD_COLS), f32),
        ),
        in_specs=[pl.BlockSpec(memory_space=pltpu.SMEM)] + [vmem] * (len(operands) - 1),
        out_specs=(vmem, vmem),
        scratch_shapes=[
            pltpu.VMEM((5, wide_rows, 2 * CH, LANES), bf16),
            pltpu.VMEM((5, mid_rows, 2 * CH, LANES), bf16),
            pltpu.VMEM((5, narrow_rows, 2 * CH, LANES), bf16),
            pltpu.VMEM((5, inner_rows, CH, LANES), bf16),
            pltpu.VMEM((mid_rows, CH, LANES), bf16),
            pltpu.VMEM((mid_rows, CH, LANES), f32),
            pltpu.VMEM((mid_rows, CH, tile), bf16),
            pltpu.VMEM((inner_rows, CH, tile), f32),
            pltpu.VMEM((inner_rows, CH, LANES), bf16),
            pltpu.VMEM((narrow_rows, CH, tile), bf16),
            pltpu.VMEM((narrow_rows, CH, LANES), bf16),
            pltpu.VMEM((narrow_rows, CH, tile), f32),
            pltpu.VMEM((narrow_rows, CH, tile), f32),
            pltpu.VMEM((2, CH, LANES), bf16),
        ],
        compiler_params=pltpu.CompilerParams(vmem_limit_bytes=48 * 1024 * 1024),
        name="blocks_backward",
    )(*operands)


def gather_sides(axis, down, up):
    devices = lax.axis_size(axis)
    before = lax.ppermute(down, axis, [(i, i + 1) for i in range(devices - 1)])
    after = lax.ppermute(up, axis, [(i + 1, i) for i in range(devices - 1)])
    return before, after


def packed(wide, narrow, last):
    rows, narrow_rows = (wide.shape[0], narrow.shape[0])
    cut = slice(-WIDE_COLS, None) if last else slice(0, WIDE_COLS)
    wide = wide[:, :, cut]
    per = 128 // WIDE_COLS
    wide = jnp.concatenate(jnp.split(wide, per, axis=0), axis=2)
    cut = slice(-NARROW_COLS, None) if last else slice(0, NARROW_COLS)
    narrow = narrow[:, :, cut]
    per = 128 // NARROW_COLS
    fill = -narrow_rows % per
    narrow = jnp.concatenate([narrow, narrow[:fill]], axis=0)
    narrow = jnp.concatenate(jnp.split(narrow, per, axis=0), axis=2)
    return jnp.concatenate([wide, narrow], axis=0)


def unpacked(message, wide_rows, narrow_rows):
    per = 128 // WIDE_COLS
    count = wide_rows // per
    wide = jnp.concatenate(jnp.split(message[:count], per, axis=2), axis=0)
    per = 128 // NARROW_COLS
    narrow = jnp.concatenate(jnp.split(message[count:], per, axis=2), axis=0)
    return wide, narrow[:narrow_rows]


def with_surroundings(band, cotangent):
    devices = lax.axis_size("off")
    mine = jnp.concatenate([band, cotangent], axis=1)
    other = lax.ppermute(mine[:, :, ::-1], "off", [(i, devices - 1 - i) for i in range(devices)])
    wide = jnp.concatenate([band, other[:, :CH]], axis=1)
    narrow = jnp.concatenate([cotangent, other[:, CH:]], axis=1)
    before, after = gather_sides(
        "pos",
        jnp.concatenate([wide[-WIDE_ROWS:], narrow[-NARROW_ROWS:]], axis=0),
        jnp.concatenate([wide[:WIDE_ROWS], narrow[:NARROW_ROWS]], axis=0),
    )
    wide = jnp.concatenate([before[:WIDE_ROWS], wide, after[:WIDE_ROWS]], axis=0)
    narrow = jnp.concatenate([before[WIDE_ROWS:], narrow, after[WIDE_ROWS:]], axis=0)
    before, after = gather_sides(
        "off", packed(wide, narrow, True), packed(wide, narrow, False)
    )
    before = unpacked(before, wide.shape[0], narrow.shape[0])
    after = unpacked(after, wide.shape[0], narrow.shape[0])
    full = []
    for tile, low, high in zip((wide, narrow), before, after):
        gap = LANES - tile.shape[2] - low.shape[2] - high.shape[2]
        zero = jnp.zeros(tile.shape[:2] + (gap,), tile.dtype)
        full.append(jnp.concatenate([tile, high, zero, low], axis=2))
    return full


def summed_over_mesh(parts):
    rows, columns = (lax.axis_size("pos"), lax.axis_size("off"))
    whole = parts.shape
    parts = parts.reshape(rows, -1)
    part = jnp.sum(lax.all_to_all(parts, "pos", 0, 0, tiled=True), axis=0)
    copies = jnp.broadcast_to(part[None], (columns,) + part.shape)
    part = jnp.sum(lax.all_to_all(copies, "off", 0, 0, tiled=True), axis=0)
    copies = jnp.broadcast_to(part[None], (rows,) + part.shape)
    return lax.all_to_all(copies, "pos", 0, 0, tiled=True).reshape(whole)


def local(band_in, conv_weight, mix_weight, norm_gain, norm_bias, cotangent):
    rows, tile = band_in.shape[1:]
    total_rows = rows * lax.axis_size("pos")
    total_cols = tile * lax.axis_size("off")
    grad_scale = 1.0 / math.sqrt(total_rows * total_cols)
    place = jnp.stack(
        [
            lax.axis_index("pos") * rows,
            lax.axis_index("off") * tile,
            jnp.int32(total_rows),
            jnp.int32(total_cols),
        ]
    )
    wide, narrow = with_surroundings(band_in.swapaxes(0, 1), cotangent.swapaxes(0, 1))
    gradient, grads = on_tile(
        wide, narrow, place, conv_weight, mix_weight, norm_gain, norm_bias, rows, tile
    )
    edge = TAPS * CH
    totals = summed_over_mesh(grads).reshape(2, CH, GRAD_COLS) * grad_scale
    conv_total = totals[:, :, :edge].reshape(2, CH, TAPS, CH).swapaxes(1, 2)
    return (
        gradient.swapaxes(0, 1),
        conv_total,
        totals[:, :, edge : edge + CH],
        totals[:, :, edge + CH],
        totals[:, :, edge + CH + 1],
    )


def solution(mesh):
    placed = (P(None, "pos", "off"), P(), P(), P(), P(), P(None, "pos", "off"))
    return jax.shard_map(
        local,
        mesh=mesh,
        in_specs=placed,
        out_specs=(P(None, "pos", "off"), P(), P(), P(), P()),
        check_vma=False,
    )
```

```python
import math

import jax
import jax.numpy as jnp
from jax import lax
from jax.experimental import pallas as pl
from jax.experimental.pallas import tpu as pltpu
from jax.sharding import PartitionSpec as P

FIRST_DILATION = 2
SECOND_DILATION = 4
CH = 32
TAPS = 9
WIDE_ROWS = 2 * (FIRST_DILATION + SECOND_DILATION)
NARROW_ROWS = FIRST_DILATION + SECOND_DILATION
WIDE_COLS = 32
NARROW_COLS = 16
LANES = 256
GRAD_COLS = 384
ACT_ROWS = 8
FIRST_ROWS = 12
SECOND_ROWS = 14
BETWEEN_ROWS = 10

SLOPE = 1.702


def tap_list(dilation):
    offsets = []
    for along_row in (-dilation, 0, dilation):
        for along_col in (-dilation, 0, dilation):
            offsets.append(((along_row + along_col) // 2, along_col - along_row))
    return offsets


def gated(values):
    half = 0.5 * values
    return half + half * jnp.tanh(SLOPE * half)


def twice_slope(halved, bent):
    return (1.0 + bent) * (1.0 + halved * (1.0 - bent))


def body(
    place,
    wide_tile,
    narrow_tile,
    before,
    after,
    conv,
    conv_back,
    conv_back_own,
    mix,
    mix_back,
    gain,
    bias,
    out,
    grads,
    act0,
    act1,
    back1,
    back0,
    mid,
    pre0,
    hid0,
    slope0,
    gsum0,
    hid1,
    gsum1,
    pre1,
    slope1,
    masks,
    sides,
    wide,
    narrow,
):
    rows = out.shape[0]
    tile = out.shape[2]
    bf16, f32 = (jnp.bfloat16, jnp.float32)
    first_row, first_col, total_rows, total_cols = [place[k] for k in range(4)]
    lane = lax.broadcasted_iota(jnp.int32, (CH, LANES), 1)
    column = first_col + jnp.where(lane < LANES - 64, lane, lane - LANES)
    masks[0] = jnp.where((column >= 0) & (column < total_cols), 1.0, 0.0).astype(bf16)
    masks[1] = jnp.where((column > 0) & (column <= total_cols), 1.0, 0.0).astype(bf16)

    side_lane = lax.broadcasted_iota(jnp.int32, (2 * CH, 128), 1)
    wide_slots = 128 // WIDE_COLS
    for base, cols in ((0, WIDE_COLS), (wide_slots, NARROW_COLS)):
        for slot in range(128 // cols):
            here = (side_lane >= slot * cols) & (side_lane < (slot + 1) * cols)
            sides[0, base + slot] = jnp.where(here, 1.0, 0.0).astype(bf16)
            sides[1, base + slot] = jnp.where(here, 0.0, 1.0).astype(bf16)
    own = slice(0, CH)

    def half_in_rows(local_row):
        row = first_row + local_row
        factor = jnp.where((row >= 0) & (row < total_rows), 0.5, 0.0)
        return jnp.broadcast_to(factor, (CH, LANES)).astype(bf16)

    def spread(target, index, values, dilation):
        stores = []
        for step in range(-2, 3):
            moved = values
            if step:
                moved = pltpu.roll(values, (-step * dilation) % LANES, 1)
            stores.append((target, (step + 2, index), moved))
        return stores

    hand_pre, hand_mix = ({}, {})

    def over_rows(count, at_once, *stages):
        def step(m, carry):
            stores = []
            for stage in stages:
                for k in range(at_once):
                    for target, index, values in stage(at_once * m + k, k):
                        if isinstance(target, dict):
                            target[index] = values
                        else:
                            stores.append((target, index, values))
            for target, index, values in stores:
                target[index] = values
            return carry

        lax.fori_loop(0, count // at_once, step, 0)

    def stacked(source, index, dilation, sign, part=slice(None), lanes=slice(None)):
        pieces = []
        for row_shift, col_shift in tap_list(dilation):
            pieces.append(
                source[sign * col_shift // dilation + 2, index + sign * row_shift, part, lanes]
            )
        return jnp.concatenate(pieces, axis=0)

    def dot(left, right):
        return jnp.dot(left, right, preferred_element_type=f32)

    def own_dot(left, right):
        return lax.dot_general(left, right, (((1,), (1,)), ((), ())), preferred_element_type=f32)

    def across(values, count=LANES):
        return jnp.concatenate([values] * (count // 128), axis=1)

    def both_halves(values):
        return jnp.concatenate([values, values], axis=0)

    def with_sides(tile_row, message, slot, cols):
        pick = slot if cols == WIDE_COLS else wide_slots + slot
        both = after[message] * sides[0, pick] + before[message] * sides[1, pick]
        if slot:
            both = pltpu.roll(both, 128 - slot * cols, 1)
        return jnp.concatenate([tile_row, both], axis=1)

    wide_messages = (rows + 2 * WIDE_ROWS) // wide_slots
    narrow_messages = before.shape[0] - wide_messages

    def fill_wide(m, carry):
        stores = []
        for k in range(ACT_ROWS):
            message = m * (ACT_ROWS // wide_slots) + k // wide_slots
            slot = k % wide_slots
            q = message + slot * wide_messages
            row = with_sides(wide_tile[q], message, slot, WIDE_COLS)
            stores.append((wide, q, row))
            stores += spread(act0, q, gated(row.astype(f32)).astype(bf16), FIRST_DILATION)
        for target, index, values in stores:
            target[index] = values
        return carry

    lax.fori_loop(0, (rows + 2 * WIDE_ROWS) // ACT_ROWS, fill_wide, 0)

    def fill_narrow(message, carry):
        for slot in range((rows + 2 * NARROW_ROWS) // narrow_messages):
            n = message + slot * narrow_messages
            narrow[n] = with_sides(
                narrow_tile[n], wide_messages + message, slot, NARROW_COLS
            )
        return carry

    lax.fori_loop(0, narrow_messages, fill_narrow, 0)

    def first_conv(n, k):
        pre = dot(conv[0], stacked(act0, n + FIRST_DILATION, FIRST_DILATION, 1))
        return [(hand_pre, k, pre)]

    def first_mix(n, k):
        pre = hand_pre[k]
        hidden = gated(across(gain[0]) * pre + across(bias[0])).astype(bf16)
        return [
            (hand_mix, k, dot(mix[0], hidden)),
            (pre0, n, pre[:CH]),
            (hid0, n, hidden[:CH, :tile]),
        ]

    def first_mirror(n, k):
        q = n + FIRST_DILATION
        summed = (wide[q].astype(f32) + hand_mix[k]).astype(bf16)
        other = pltpu.roll(summed[CH:], 1, 1)
        both = (summed[:CH] * masks[0] + other * masks[1]) * half_in_rows(q - WIDE_ROWS)
        act = gated(both.astype(f32)).astype(bf16)
        acts = jnp.concatenate([act * masks[0], act * masks[1]], axis=0)
        return spread(act1, n, acts, SECOND_DILATION) + [(mid, n, both)]

    over_rows(
        rows + 2 * (WIDE_ROWS - FIRST_DILATION), FIRST_ROWS, first_conv, first_mix, first_mirror
    )

    def second_conv(n, k):
        pre = dot(conv[1], stacked(act1, n + SECOND_DILATION, SECOND_DILATION, 1))
        cot = narrow[n]
        total = (cot[:CH] + pltpu.roll(cot[CH:], 1, 1)) * jnp.asarray(0.5, bf16)
        sides = jnp.concatenate([total * masks[0], total * masks[1]], axis=0)
        return [
            (hand_pre, k, pre),
            (hand_mix, k, dot(mix_back[1], sides)),
            (gsum1, n, total),
        ]

    def second_slope(n, k):
        pre = hand_pre[k]
        halved = (0.5 * SLOPE) * (across(gain[1]) * pre + across(bias[1]))
        bent = jnp.tanh(halved)
        grad_pre = hand_mix[k] * twice_slope(halved, bent)
        hidden = (halved[:CH, :tile] * (1.0 / SLOPE)) * (1.0 + bent[:CH, :tile])
        grad_conv = (grad_pre * across(gain[1])).astype(bf16)
        return spread(back1, n, grad_conv, SECOND_DILATION) + [
            (pre1, n, pre[:CH, :tile]),
            (slope1, n, grad_pre[:CH, :tile]),
            (hid1, n, hidden.astype(bf16)),
        ]

    over_rows(rows + 2 * NARROW_ROWS, SECOND_ROWS, second_conv, second_slope)

    def between_conv(n, k):
        rows_at = n + SECOND_DILATION
        return [(hand_pre, k, dot(conv_back[...], stacked(back1, rows_at, SECOND_DILATION, -1)))]

    def between_mirror(n, k):
        halved = (0.5 * SLOPE) * mid[n + NARROW_ROWS + FIRST_DILATION].astype(f32)
        slope = twice_slope(halved, jnp.tanh(halved))
        total = gsum1[n + SECOND_DILATION].astype(f32)
        grad_in = (both_halves(total) + both_halves(slope) * hand_pre[k]).astype(bf16)
        both = grad_in[:CH] * masks[0] + grad_in[CH:] * masks[1]
        both = (both * masks[0]) * half_in_rows(n - FIRST_DILATION)
        return [(hand_mix, (k, own), dot(mix_back[0, :CH, :CH], both)), (gsum0, n, both)]

    def between_slope(n, k):
        pre = pre0[n + WIDE_ROWS - 2 * FIRST_DILATION]
        halved = (0.5 * SLOPE) * (across(gain[0, :CH]) * pre + across(bias[0, :CH]))
        grad_pre = hand_mix[k, own] * twice_slope(halved, jnp.tanh(halved))
        grad_conv = (grad_pre * across(gain[0, :CH])).astype(bf16)
        return spread(back0, n, grad_conv, FIRST_DILATION) + [(slope0, n, grad_pre[:, :tile])]

    over_rows(
        rows + 2 * FIRST_DILATION, BETWEEN_ROWS, between_conv, between_mirror, between_slope
    )

    near = slice(0, tile)

    def finish(m, carry):
        conv0, conv1, mix0, mix1, gain0, bias0, gain1, bias1 = carry

        def pair(load):
            return jnp.concatenate([load(2 * m), load(2 * m + 1)], axis=1)

        back = dot(
            conv_back_own[...],
            pair(lambda n: stacked(back0, n + FIRST_DILATION, FIRST_DILATION, -1, own, near)),
        )
        values = pair(lambda n: wide[n + WIDE_ROWS, own, near]).astype(f32)
        halved = (0.5 * SLOPE) * values
        total0 = pair(lambda n: gsum0[n + FIRST_DILATION, :, near])
        result = total0.astype(f32) + twice_slope(halved, jnp.tanh(halved)) * back
        result = result.astype(bf16)
        out[2 * m] = result[:, :tile]
        out[2 * m + 1] = result[:, tile:]
        grad0 = pair(lambda n: back0[2, n + FIRST_DILATION, :, near])
        grad1 = pair(lambda n: back1[2, n + NARROW_ROWS, own, near])
        stack0 = pair(lambda n: stacked(act0, n + WIDE_ROWS, FIRST_DILATION, 1, own, near))
        stack1 = pair(
            lambda n: stacked(
                act1, n + WIDE_ROWS - FIRST_DILATION, SECOND_DILATION, 1, own, near
            )
        )
        conv0 = conv0 + own_dot(grad0, stack0)
        conv1 = conv1 + own_dot(grad1, stack1)
        mix0 = mix0 + own_dot(total0, pair(lambda n: hid0[n + WIDE_ROWS - FIRST_DILATION]))
        total1 = pair(lambda n: gsum1[n + NARROW_ROWS, :, near])
        mix1 = mix1 + own_dot(total1, pair(lambda n: hid1[n + NARROW_ROWS]))
        for n in (2 * m, 2 * m + 1):
            grad = slope0[n + FIRST_DILATION]
            bias0 = bias0 + grad
            gain0 = gain0 + grad * pre0[n + WIDE_ROWS - FIRST_DILATION, :, near]
            grad = slope1[n + NARROW_ROWS]
            bias1 = bias1 + grad
            gain1 = gain1 + grad * pre1[n + NARROW_ROWS]
        return conv0, conv1, mix0, mix1, gain0, bias0, gain1, bias1

    taps_zero = jnp.zeros((CH, TAPS * CH), f32)
    small_zero = jnp.zeros((CH, CH), f32)
    tile_zero = jnp.zeros((CH, tile), f32)
    start = (taps_zero,) * 2 + (small_zero,) * 2 + (tile_zero,) * 4
    conv0, conv1, mix0, mix1, gain0, bias0, gain1, bias1 = lax.fori_loop(
        0, rows // 2, finish, start, unroll=2
    )
    edge = TAPS * CH
    for s, parts in enumerate(((conv0, mix0, gain0, bias0), (conv1, mix1, gain1, bias1))):
        place_s = slice(s * CH, (s + 1) * CH)
        grads[place_s, 0:edge] = parts[0]
        sums = [jnp.sum(part, axis=1, keepdims=True) for part in parts[2:]]
        rest = jnp.zeros((CH, GRAD_COLS - edge - CH - 2), f32)
        grads[place_s, edge:] = jnp.concatenate([parts[1]] + sums + [rest], axis=1)


def swap_mesh_tap(weights):
    return weights.reshape((3, 3) + weights.shape[1:]).swapaxes(0, 1).reshape(weights.shape)


def two_sided(weights):
    other = swap_mesh_tap(weights)
    zero = jnp.zeros_like(weights)
    top = jnp.concatenate([weights, zero], axis=2)
    low = jnp.concatenate([zero, other], axis=2)
    both = jnp.concatenate([top, low], axis=1)
    return both.transpose(1, 0, 2).reshape(2 * CH, TAPS * 2 * CH)


def two_diagonal(weights):
    zero = jnp.zeros_like(weights)
    top = jnp.concatenate([weights, zero], axis=2)
    return jnp.concatenate([top, jnp.concatenate([zero, weights], axis=2)], axis=1)


def on_tile(fields, place, conv_weight, mix_weight, norm_gain, norm_bias, rows, tile):
    bf16, f32 = (jnp.bfloat16, jnp.float32)
    back = 0.5 * conv_weight.swapaxes(2, 3)

    def per_channel(values):
        return jnp.broadcast_to(jnp.tile(values, (1, 2))[:, :, None], (2, 2 * CH, 128))

    operands = (
        place,
        *fields,
        jnp.stack([two_sided(conv_weight[s]) for s in range(2)]),
        two_sided(back[1]),
        back[0].transpose(1, 0, 2).reshape(CH, TAPS * CH),
        two_diagonal(mix_weight),
        two_diagonal(0.5 * mix_weight.swapaxes(1, 2)),
        per_channel(norm_gain),
        per_channel(norm_bias),
    )
    wide_rows = rows + 2 * WIDE_ROWS
    mid_rows = wide_rows - 2 * FIRST_DILATION
    narrow_rows = rows + 2 * NARROW_ROWS
    inner_rows = rows + 2 * FIRST_DILATION
    vmem = pl.BlockSpec(memory_space=pltpu.VMEM)
    return pl.pallas_call(
        body,
        out_shape=(
            jax.ShapeDtypeStruct((rows, CH, tile), bf16),
            jax.ShapeDtypeStruct((2 * CH, GRAD_COLS), f32),
        ),
        in_specs=[pl.BlockSpec(memory_space=pltpu.SMEM)] + [vmem] * (len(operands) - 1),
        out_specs=(vmem, vmem),
        scratch_shapes=[
            pltpu.VMEM((5, wide_rows, 2 * CH, LANES), bf16),
            pltpu.VMEM((5, mid_rows, 2 * CH, LANES), bf16),
            pltpu.VMEM((5, narrow_rows, 2 * CH, LANES), bf16),
            pltpu.VMEM((5, inner_rows, CH, LANES), bf16),
            pltpu.VMEM((mid_rows, CH, LANES), bf16),
            pltpu.VMEM((mid_rows, CH, LANES), f32),
            pltpu.VMEM((mid_rows, CH, tile), bf16),
            pltpu.VMEM((inner_rows, CH, tile), f32),
            pltpu.VMEM((inner_rows, CH, LANES), bf16),
            pltpu.VMEM((narrow_rows, CH, tile), bf16),
            pltpu.VMEM((narrow_rows, CH, LANES), bf16),
            pltpu.VMEM((narrow_rows, CH, tile), f32),
            pltpu.VMEM((narrow_rows, CH, tile), f32),
            pltpu.VMEM((2, CH, LANES), bf16),
            pltpu.VMEM((2, 128 // WIDE_COLS + 128 // NARROW_COLS, 2 * CH, 128), bf16),
            pltpu.VMEM((wide_rows, 2 * CH, LANES), bf16),
            pltpu.VMEM((narrow_rows, 2 * CH, LANES), bf16),
        ],
        compiler_params=pltpu.CompilerParams(vmem_limit_bytes=48 * 1024 * 1024),
        name="blocks_backward",
    )(*operands)


def gather_sides(axis, down, up):
    devices = lax.axis_size(axis)
    before = lax.ppermute(down, axis, [(i, i + 1) for i in range(devices - 1)])
    after = lax.ppermute(up, axis, [(i + 1, i) for i in range(devices - 1)])
    return before, after


def packed(wide, narrow, last):
    def in_slots(rows, cols):
        slots = 128 // cols
        edge = rows[:, :, -cols:] if last else rows[:, :, :cols]
        edge = jnp.concatenate([edge, edge[: -rows.shape[0] % slots]], axis=0)
        pieces = jnp.split(edge, slots, axis=0)
        if last:
            pieces = pieces[1:] + pieces[:1]
        return jnp.concatenate(pieces, axis=2)

    return jnp.concatenate([in_slots(wide, WIDE_COLS), in_slots(narrow, NARROW_COLS)], axis=0)


def with_surroundings(band, cotangent):
    devices = lax.axis_size("off")
    mine = jnp.concatenate([band, cotangent], axis=1)
    other = lax.ppermute(mine[:, :, ::-1], "off", [(i, devices - 1 - i) for i in range(devices)])
    wide = jnp.concatenate([band, other[:, :CH]], axis=1)
    narrow = jnp.concatenate([cotangent, other[:, CH:]], axis=1)
    before, after = gather_sides(
        "pos",
        jnp.concatenate([wide[-WIDE_ROWS:], narrow[-NARROW_ROWS:]], axis=0),
        jnp.concatenate([wide[:WIDE_ROWS], narrow[:NARROW_ROWS]], axis=0),
    )
    wide = jnp.concatenate([before[:WIDE_ROWS], wide, after[:WIDE_ROWS]], axis=0)
    narrow = jnp.concatenate([before[WIDE_ROWS:], narrow, after[WIDE_ROWS:]], axis=0)
    before, after = gather_sides(
        "off", packed(wide, narrow, True), packed(wide, narrow, False)
    )
    return wide, narrow, before, after


def summed_over_mesh(parts):
    rows, columns = (lax.axis_size("pos"), lax.axis_size("off"))
    size = 2 * columns
    near = [[size * g + i for i in range(size)] for g in range(rows // 2)]
    far = [[2 * g + i for g in range(rows // 2)] for i in range(2)]
    axes = ("pos", "off")

    def exchanged(blocks, axis, groups):
        return lax.all_to_all(blocks, axis, 0, 0, tiled=True, axis_index_groups=groups)

    def copies(part, count):
        return jnp.broadcast_to(part[None], (count,) + part.shape)

    blocks = parts.reshape(size, -1, parts.shape[1])
    part = jnp.sum(exchanged(blocks, axes, near), axis=0)
    part = jnp.sum(exchanged(copies(part, rows // 2), "pos", far), axis=0)
    return exchanged(copies(part, size), axes, near).reshape(parts.shape)


def local(band_in, conv_weight, mix_weight, norm_gain, norm_bias, cotangent):
    rows, tile = band_in.shape[1:]
    total_rows = rows * lax.axis_size("pos")
    total_cols = tile * lax.axis_size("off")
    grad_scale = 1.0 / math.sqrt(total_rows * total_cols)
    place = jnp.stack(
        [
            lax.axis_index("pos") * rows,
            lax.axis_index("off") * tile,
            jnp.int32(total_rows),
            jnp.int32(total_cols),
        ]
    )
    fields = with_surroundings(band_in.swapaxes(0, 1), cotangent.swapaxes(0, 1))
    gradient, grads = on_tile(
        fields, place, conv_weight, mix_weight, norm_gain, norm_bias, rows, tile
    )
    edge = TAPS * CH
    totals = summed_over_mesh(grads).reshape(2, CH, GRAD_COLS) * grad_scale
    conv_total = totals[:, :, :edge].reshape(2, CH, TAPS, CH).swapaxes(1, 2)
    return (
        gradient.swapaxes(0, 1),
        conv_total,
        totals[:, :, edge : edge + CH],
        totals[:, :, edge + CH],
        totals[:, :, edge + CH + 1],
    )


def solution(mesh):
    placed = (P(None, "pos", "off"), P(), P(), P(), P(), P(None, "pos", "off"))
    return jax.shard_map(
        local,
        mesh=mesh,
        in_specs=placed,
        out_specs=(P(None, "pos", "off"), P(), P(), P(), P()),
        check_vma=False,
    )
```

```python
import functools
import math

import jax
import jax.numpy as jnp
from jax import lax
from jax.experimental import pallas as pl
from jax.experimental.pallas import tpu as pltpu
from jax.sharding import PartitionSpec as P

FIRST_DILATION = 2
SECOND_DILATION = 4
CH = 32
TAPS = 9
WIDE_ROWS = 2 * (FIRST_DILATION + SECOND_DILATION)
NARROW_ROWS = FIRST_DILATION + SECOND_DILATION
WIDE_COLS = 32
NARROW_COLS = 16
LANES = 256
GRAD_COLS = 384
ACT_ROWS = 8
FIRST_ROWS = 12
SECOND_ROWS = 14
BETWEEN_ROWS = 10

SLOPE = 1.702


def tap_list(dilation):
    offsets = []
    for along_row in (-dilation, 0, dilation):
        for along_col in (-dilation, 0, dilation):
            offsets.append(((along_row + along_col) // 2, along_col - along_row))
    return offsets


def gated(values):
    half = 0.5 * values
    return half + half * jnp.tanh(SLOPE * half)


def twice_slope(halved, bent):
    return (1.0 + bent) * (1.0 + halved * (1.0 - bent))


def body(
    place,
    wide_tile,
    narrow_tile,
    before,
    after,
    conv,
    conv_back,
    conv_back_own,
    mix,
    mix_back,
    gain,
    bias,
    out,
    grads,
    act0,
    act1,
    back1,
    back0,
    mid,
    pre0,
    hid0,
    slope0,
    gsum0,
    hid1,
    gsum1,
    pre1,
    slope1,
    masks,
    sides,
    wide,
    narrow,
):
    rows = out.shape[0]
    tile = out.shape[2]
    bf16, f32 = (jnp.bfloat16, jnp.float32)
    first_row, first_col, total_rows, total_cols = [place[k] for k in range(4)]
    lane = lax.broadcasted_iota(jnp.int32, (CH, LANES), 1)
    column = first_col + jnp.where(lane < LANES - 64, lane, lane - LANES)
    masks[0] = jnp.where((column >= 0) & (column < total_cols), 1.0, 0.0).astype(bf16)
    masks[1] = jnp.where((column > 0) & (column <= total_cols), 1.0, 0.0).astype(bf16)

    side_lane = lax.broadcasted_iota(jnp.int32, (2 * CH, 128), 1)
    wide_slots = 128 // WIDE_COLS
    for base, cols in ((0, WIDE_COLS), (wide_slots, NARROW_COLS)):
        for slot in range(128 // cols):
            here = (side_lane >= slot * cols) & (side_lane < (slot + 1) * cols)
            sides[0, base + slot] = jnp.where(here, 1.0, 0.0).astype(bf16)
            sides[1, base + slot] = jnp.where(here, 0.0, 1.0).astype(bf16)
    own = slice(0, CH)

    def half_in_rows(local_row):
        row = first_row + local_row
        factor = jnp.where((row >= 0) & (row < total_rows), 0.5, 0.0)
        return jnp.broadcast_to(factor, (CH, LANES)).astype(bf16)

    def spread(target, index, values, dilation):
        stores = []
        for step in range(-2, 3):
            moved = values
            if step:
                moved = pltpu.roll(values, (-step * dilation) % LANES, 1)
            stores.append((target, (step + 2, index), moved))
        return stores

    hand_pre, hand_mix = ({}, {})

    def over_rows(count, at_once, *stages):
        def step(m, carry):
            stores = []
            for stage in stages:
                for k in range(at_once):
                    for target, index, values in stage(at_once * m + k, k):
                        if isinstance(target, dict):
                            target[index] = values
                        else:
                            stores.append((target, index, values))
            for target, index, values in stores:
                target[index] = values
            return carry

        lax.fori_loop(0, count // at_once, step, 0)

    def stacked(source, index, dilation, sign, part=slice(None), lanes=slice(None)):
        pieces = []
        for row_shift, col_shift in tap_list(dilation):
            pieces.append(
                source[sign * col_shift // dilation + 2, index + sign * row_shift, part, lanes]
            )
        return jnp.concatenate(pieces, axis=0)

    def dot(left, right):
        return jnp.dot(left, right, preferred_element_type=f32)

    def own_dot(left, right):
        return lax.dot_general(left, right, (((1,), (1,)), ((), ())), preferred_element_type=f32)

    def across(values, count=LANES):
        return jnp.concatenate([values] * (count // 128), axis=1)

    def both_halves(values):
        return jnp.concatenate([values, values], axis=0)

    def with_sides(tile_row, message, slot, cols):
        pick = slot if cols == WIDE_COLS else wide_slots + slot
        both = after[message] * sides[0, pick] + before[message] * sides[1, pick]
        if slot:
            both = pltpu.roll(both, 128 - slot * cols, 1)
        return jnp.concatenate([tile_row, both], axis=1)

    wide_messages = (rows + 2 * WIDE_ROWS) // wide_slots
    narrow_messages = before.shape[0] - wide_messages

    def fill_wide(m, carry):
        stores = []
        for k in range(ACT_ROWS):
            message = m * (ACT_ROWS // wide_slots) + k // wide_slots
            slot = k % wide_slots
            q = message + slot * wide_messages
            row = with_sides(wide_tile[q], message, slot, WIDE_COLS)
            stores.append((wide, q, row))
            stores += spread(act0, q, gated(row.astype(f32)).astype(bf16), FIRST_DILATION)
        for target, index, values in stores:
            target[index] = values
        return carry

    lax.fori_loop(0, (rows + 2 * WIDE_ROWS) // ACT_ROWS, fill_wide, 0)

    def fill_narrow(message, carry):
        for slot in range((rows + 2 * NARROW_ROWS) // narrow_messages):
            n = message + slot * narrow_messages
            narrow[n] = with_sides(
                narrow_tile[n], wide_messages + message, slot, NARROW_COLS
            )
        return carry

    lax.fori_loop(0, narrow_messages, fill_narrow, 0)

    def first_conv(n, k):
        pre = dot(conv[0], stacked(act0, n + FIRST_DILATION, FIRST_DILATION, 1))
        return [(hand_pre, k, pre)]

    def first_mix(n, k):
        pre = hand_pre[k]
        hidden = gated(across(gain[0]) * pre + across(bias[0])).astype(bf16)
        return [
            (hand_mix, k, dot(mix[0], hidden)),
            (pre0, n, pre[:CH]),
            (hid0, n, hidden[:CH, :tile]),
        ]

    def first_mirror(n, k):
        q = n + FIRST_DILATION
        summed = (wide[q].astype(f32) + hand_mix[k]).astype(bf16)
        other = pltpu.roll(summed[CH:], 1, 1)
        both = (summed[:CH] * masks[0] + other * masks[1]) * half_in_rows(q - WIDE_ROWS)
        act = gated(both.astype(f32)).astype(bf16)
        acts = jnp.concatenate([act * masks[0], act * masks[1]], axis=0)
        return spread(act1, n, acts, SECOND_DILATION) + [(mid, n, both)]

    over_rows(
        rows + 2 * (WIDE_ROWS - FIRST_DILATION), FIRST_ROWS, first_conv, first_mix, first_mirror
    )

    def second_conv(n, k):
        pre = dot(conv[1], stacked(act1, n + SECOND_DILATION, SECOND_DILATION, 1))
        cot = narrow[n]
        total = (cot[:CH] + pltpu.roll(cot[CH:], 1, 1)) * jnp.asarray(0.5, bf16)
        sides = jnp.concatenate([total * masks[0], total * masks[1]], axis=0)
        return [
            (hand_pre, k, pre),
            (hand_mix, k, dot(mix_back[1], sides)),
            (gsum1, n, total),
        ]

    def second_slope(n, k):
        pre = hand_pre[k]
        halved = (0.5 * SLOPE) * (across(gain[1]) * pre + across(bias[1]))
        bent = jnp.tanh(halved)
        grad_pre = hand_mix[k] * twice_slope(halved, bent)
        hidden = (halved[:CH, :tile] * (1.0 / SLOPE)) * (1.0 + bent[:CH, :tile])
        grad_conv = (grad_pre * across(gain[1])).astype(bf16)
        return spread(back1, n, grad_conv, SECOND_DILATION) + [
            (pre1, n, pre[:CH, :tile]),
            (slope1, n, grad_pre[:CH, :tile]),
            (hid1, n, hidden.astype(bf16)),
        ]

    over_rows(rows + 2 * NARROW_ROWS, SECOND_ROWS, second_conv, second_slope)

    def between_conv(n, k):
        rows_at = n + SECOND_DILATION
        return [(hand_pre, k, dot(conv_back[...], stacked(back1, rows_at, SECOND_DILATION, -1)))]

    def between_mirror(n, k):
        halved = (0.5 * SLOPE) * mid[n + NARROW_ROWS + FIRST_DILATION].astype(f32)
        slope = twice_slope(halved, jnp.tanh(halved))
        total = gsum1[n + SECOND_DILATION].astype(f32)
        grad_in = (both_halves(total) + both_halves(slope) * hand_pre[k]).astype(bf16)
        both = grad_in[:CH] * masks[0] + grad_in[CH:] * masks[1]
        both = (both * masks[0]) * half_in_rows(n - FIRST_DILATION)
        return [(hand_mix, (k, own), dot(mix_back[0, :CH, :CH], both)), (gsum0, n, both)]

    def between_slope(n, k):
        pre = pre0[n + WIDE_ROWS - 2 * FIRST_DILATION]
        halved = (0.5 * SLOPE) * (across(gain[0, :CH]) * pre + across(bias[0, :CH]))
        grad_pre = hand_mix[k, own] * twice_slope(halved, jnp.tanh(halved))
        grad_conv = (grad_pre * across(gain[0, :CH])).astype(bf16)
        return spread(back0, n, grad_conv, FIRST_DILATION) + [(slope0, n, grad_pre[:, :tile])]

    over_rows(
        rows + 2 * FIRST_DILATION, BETWEEN_ROWS, between_conv, between_mirror, between_slope
    )

    near = slice(0, tile)

    def finish(m, carry):
        conv0, conv1, mix0, mix1, gain0, bias0, gain1, bias1 = carry

        def pair(load):
            return jnp.concatenate([load(2 * m), load(2 * m + 1)], axis=1)

        back = dot(
            conv_back_own[...],
            pair(lambda n: stacked(back0, n + FIRST_DILATION, FIRST_DILATION, -1, own, near)),
        )
        values = pair(lambda n: wide[n + WIDE_ROWS, own, near]).astype(f32)
        halved = (0.5 * SLOPE) * values
        total0 = pair(lambda n: gsum0[n + FIRST_DILATION, :, near])
        result = total0.astype(f32) + twice_slope(halved, jnp.tanh(halved)) * back
        result = result.astype(bf16)
        out[2 * m] = result[:, :tile]
        out[2 * m + 1] = result[:, tile:]
        grad0 = pair(lambda n: back0[2, n + FIRST_DILATION, :, near])
        grad1 = pair(lambda n: back1[2, n + NARROW_ROWS, own, near])
        stack0 = pair(lambda n: stacked(act0, n + WIDE_ROWS, FIRST_DILATION, 1, own, near))
        stack1 = pair(
            lambda n: stacked(
                act1, n + WIDE_ROWS - FIRST_DILATION, SECOND_DILATION, 1, own, near
            )
        )
        conv0 = conv0 + own_dot(grad0, stack0)
        conv1 = conv1 + own_dot(grad1, stack1)
        mix0 = mix0 + own_dot(total0, pair(lambda n: hid0[n + WIDE_ROWS - FIRST_DILATION]))
        total1 = pair(lambda n: gsum1[n + NARROW_ROWS, :, near])
        mix1 = mix1 + own_dot(total1, pair(lambda n: hid1[n + NARROW_ROWS]))
        for n in (2 * m, 2 * m + 1):
            grad = slope0[n + FIRST_DILATION]
            bias0 = bias0 + grad
            gain0 = gain0 + grad * pre0[n + WIDE_ROWS - FIRST_DILATION, :, near]
            grad = slope1[n + NARROW_ROWS]
            bias1 = bias1 + grad
            gain1 = gain1 + grad * pre1[n + NARROW_ROWS]
        return conv0, conv1, mix0, mix1, gain0, bias0, gain1, bias1

    taps_zero = jnp.zeros((CH, TAPS * CH), f32)
    small_zero = jnp.zeros((CH, CH), f32)
    tile_zero = jnp.zeros((CH, tile), f32)
    start = (taps_zero,) * 2 + (small_zero,) * 2 + (tile_zero,) * 4
    conv0, conv1, mix0, mix1, gain0, bias0, gain1, bias1 = lax.fori_loop(
        0, rows // 2, finish, start, unroll=2
    )
    edge = TAPS * CH
    for s, parts in enumerate(((conv0, mix0, gain0, bias0), (conv1, mix1, gain1, bias1))):
        place_s = slice(s * CH, (s + 1) * CH)
        grads[place_s, 0:edge] = parts[0]
        sums = [jnp.sum(part, axis=1, keepdims=True) for part in parts[2:]]
        rest = jnp.zeros((CH, GRAD_COLS - edge - CH - 2), f32)
        grads[place_s, edge:] = jnp.concatenate([parts[1]] + sums + [rest], axis=1)


def swap_mesh_tap(weights):
    return weights.reshape((3, 3) + weights.shape[1:]).swapaxes(0, 1).reshape(weights.shape)


def two_sided(weights):
    other = swap_mesh_tap(weights)
    zero = jnp.zeros_like(weights)
    top = jnp.concatenate([weights, zero], axis=2)
    low = jnp.concatenate([zero, other], axis=2)
    both = jnp.concatenate([top, low], axis=1)
    return both.transpose(1, 0, 2).reshape(2 * CH, TAPS * 2 * CH)


def two_diagonal(weights):
    zero = jnp.zeros_like(weights)
    top = jnp.concatenate([weights, zero], axis=2)
    return jnp.concatenate([top, jnp.concatenate([zero, weights], axis=2)], axis=1)


def on_tile(fields, place, conv_weight, mix_weight, norm_gain, norm_bias, rows, tile):
    bf16, f32 = (jnp.bfloat16, jnp.float32)
    back = 0.5 * conv_weight.swapaxes(2, 3)

    def per_channel(values):
        return jnp.broadcast_to(jnp.tile(values, (1, 2))[:, :, None], (2, 2 * CH, 128))

    operands = (
        place,
        *fields,
        jnp.stack([two_sided(conv_weight[s]) for s in range(2)]),
        two_sided(back[1]),
        back[0].transpose(1, 0, 2).reshape(CH, TAPS * CH),
        two_diagonal(mix_weight),
        two_diagonal(0.5 * mix_weight.swapaxes(1, 2)),
        per_channel(norm_gain),
        per_channel(norm_bias),
    )
    wide_rows = rows + 2 * WIDE_ROWS
    mid_rows = wide_rows - 2 * FIRST_DILATION
    narrow_rows = rows + 2 * NARROW_ROWS
    inner_rows = rows + 2 * FIRST_DILATION
    vmem = pl.BlockSpec(memory_space=pltpu.VMEM)
    return pl.pallas_call(
        body,
        out_shape=(
            jax.ShapeDtypeStruct((rows, CH, tile), bf16),
            jax.ShapeDtypeStruct((2 * CH, GRAD_COLS), f32),
        ),
        in_specs=[pl.BlockSpec(memory_space=pltpu.SMEM)] + [vmem] * (len(operands) - 1),
        out_specs=(vmem, vmem),
        scratch_shapes=[
            pltpu.VMEM((5, wide_rows, 2 * CH, LANES), bf16),
            pltpu.VMEM((5, mid_rows, 2 * CH, LANES), bf16),
            pltpu.VMEM((5, narrow_rows, 2 * CH, LANES), bf16),
            pltpu.VMEM((5, inner_rows, CH, LANES), bf16),
            pltpu.VMEM((mid_rows, CH, LANES), bf16),
            pltpu.VMEM((mid_rows, CH, LANES), f32),
            pltpu.VMEM((mid_rows, CH, tile), bf16),
            pltpu.VMEM((inner_rows, CH, tile), f32),
            pltpu.VMEM((inner_rows, CH, LANES), bf16),
            pltpu.VMEM((narrow_rows, CH, tile), bf16),
            pltpu.VMEM((narrow_rows, CH, LANES), bf16),
            pltpu.VMEM((narrow_rows, CH, tile), f32),
            pltpu.VMEM((narrow_rows, CH, tile), f32),
            pltpu.VMEM((2, CH, LANES), bf16),
            pltpu.VMEM((2, 128 // WIDE_COLS + 128 // NARROW_COLS, 2 * CH, 128), bf16),
            pltpu.VMEM((wide_rows, 2 * CH, LANES), bf16),
            pltpu.VMEM((narrow_rows, 2 * CH, LANES), bf16),
        ],
        compiler_params=pltpu.CompilerParams(vmem_limit_bytes=48 * 1024 * 1024),
        name="blocks_backward",
    )(*operands)


def gather_sides(axis, down, up):
    devices = lax.axis_size(axis)
    odd = lax.axis_index(axis) % 2 == 1
    routes = []
    for start in (0, 1):
        pairs = [(i, i + 1) for i in range(start, devices - 1, 2)]
        routes.append(pairs + [(j, i) for i, j in pairs])
    within = lax.ppermute(jnp.where(odd, up, down), axis, routes[0])
    across = lax.ppermute(jnp.where(odd, down, up), axis, routes[1])
    return jnp.where(odd, within, across), jnp.where(odd, across, within)


def packed(wide, narrow, last):
    def in_slots(rows, cols):
        slots = 128 // cols
        edge = rows[:, :, -cols:] if last else rows[:, :, :cols]
        edge = jnp.concatenate([edge, edge[: -rows.shape[0] % slots]], axis=0)
        pieces = jnp.split(edge, slots, axis=0)
        if last:
            pieces = pieces[1:] + pieces[:1]
        return jnp.concatenate(pieces, axis=2)

    return jnp.concatenate([in_slots(wide, WIDE_COLS), in_slots(narrow, NARROW_COLS)], axis=0)


def with_surroundings(band, cotangent):
    devices = lax.axis_size("off")
    mine = jnp.concatenate([band, cotangent], axis=1)
    other = lax.ppermute(mine[:, :, ::-1], "off", [(i, devices - 1 - i) for i in range(devices)])
    wide = jnp.concatenate([band, other[:, :CH]], axis=1)
    narrow = jnp.concatenate([cotangent, other[:, CH:]], axis=1)
    before, after = gather_sides(
        "pos",
        jnp.concatenate([wide[-WIDE_ROWS:], narrow[-NARROW_ROWS:]], axis=0),
        jnp.concatenate([wide[:WIDE_ROWS], narrow[:NARROW_ROWS]], axis=0),
    )
    wide = jnp.concatenate([before[:WIDE_ROWS], wide, after[:WIDE_ROWS]], axis=0)
    narrow = jnp.concatenate([before[WIDE_ROWS:], narrow, after[WIDE_ROWS:]], axis=0)
    before, after = gather_sides(
        "off", packed(wide, narrow, True), packed(wide, narrow, False)
    )
    return wide, narrow, before, after


def unpack(scale, blocks, conv, mix, gain, bias, grads):
    edge = TAPS * CH
    count, height = blocks.shape[:2]
    for k in range(count):
        grads[k * height : (k + 1) * height] = blocks[k]
    for s in range(2):
        part = slice(s * CH, (s + 1) * CH)
        for tap in range(TAPS):
            conv[s, tap] = grads[part, tap * CH : (tap + 1) * CH] * scale
        mix[s] = grads[part, edge : edge + CH] * scale
        rest = (grads[part, 2 * 128 : 3 * 128] * scale).T
        start = edge + CH - 2 * 128
        gain[s : s + 1] = rest[start : start + 1]
        bias[s : s + 1] = rest[start + 1 : start + 2]


def unpacked(blocks, scale):
    f32 = jnp.float32
    vmem = pl.BlockSpec(memory_space=pltpu.VMEM)
    return pl.pallas_call(
        functools.partial(unpack, scale),
        out_shape=(
            jax.ShapeDtypeStruct((2, TAPS, CH, CH), f32),
            jax.ShapeDtypeStruct((2, CH, CH), f32),
            jax.ShapeDtypeStruct((2, CH), f32),
            jax.ShapeDtypeStruct((2, CH), f32),
        ),
        in_specs=[vmem],
        out_specs=(vmem,) * 4,
        scratch_shapes=[pltpu.VMEM((2 * CH, GRAD_COLS), f32)],
        name="unpack_gradients",
    )(blocks)


def summed_over_mesh(parts):
    rows, columns = (lax.axis_size("pos"), lax.axis_size("off"))
    size = 2 * columns
    near = [[size * g + i for i in range(size)] for g in range(rows // 2)]
    far = [[2 * g + i for g in range(rows // 2)] for i in range(2)]
    axes = ("pos", "off")

    def exchanged(blocks, axis, groups):
        return lax.all_to_all(blocks, axis, 0, 0, tiled=True, axis_index_groups=groups)

    def copies(part, count):
        return jnp.broadcast_to(part[None], (count,) + part.shape)

    blocks = parts.reshape(size, -1, parts.shape[1])
    part = jnp.sum(exchanged(blocks, axes, near), axis=0)
    part = exchanged(copies(part.astype(jnp.bfloat16), rows // 2), "pos", far)
    part = jnp.sum(part.astype(jnp.float32), axis=0)
    return exchanged(copies(part, size), axes, near)


def local(band_in, conv_weight, mix_weight, norm_gain, norm_bias, cotangent):
    rows, tile = band_in.shape[1:]
    total_rows = rows * lax.axis_size("pos")
    total_cols = tile * lax.axis_size("off")
    grad_scale = 1.0 / math.sqrt(total_rows * total_cols)
    place = jnp.stack(
        [
            lax.axis_index("pos") * rows,
            lax.axis_index("off") * tile,
            jnp.int32(total_rows),
            jnp.int32(total_cols),
        ]
    )
    fields = with_surroundings(band_in.swapaxes(0, 1), cotangent.swapaxes(0, 1))
    gradient, grads = on_tile(
        fields, place, conv_weight, mix_weight, norm_gain, norm_bias, rows, tile
    )
    return (gradient.swapaxes(0, 1), *unpacked(summed_over_mesh(grads), grad_scale))


def solution(mesh):
    placed = (P(None, "pos", "off"), P(), P(), P(), P(), P(None, "pos", "off"))
    return jax.shard_map(
        local,
        mesh=mesh,
        in_specs=placed,
        out_specs=(P(None, "pos", "off"), P(), P(), P(), P()),
        check_vma=False,
    )
```

```python
import functools
import math

import jax
import jax.numpy as jnp
from jax import lax
from jax.experimental import pallas as pl
from jax.experimental.pallas import tpu as pltpu
from jax.sharding import PartitionSpec as P

FIRST_DILATION = 2
SECOND_DILATION = 4
CH = 32
TAPS = 9
WIDE_ROWS = 2 * (FIRST_DILATION + SECOND_DILATION)
NARROW_ROWS = FIRST_DILATION + SECOND_DILATION
WIDE_COLS = 25
NARROW_COLS = 16
LANES = 256
GRAD_COLS = 384
ACT_ROWS = 10
FIRST_ROWS = 18
SECOND_ROWS = 14
BETWEEN_ROWS = 10

SLOPE = 1.702


def tap_list(dilation):
    offsets = []
    for along_row in (-dilation, 0, dilation):
        for along_col in (-dilation, 0, dilation):
            offsets.append(((along_row + along_col) // 2, along_col - along_row))
    return offsets


def gated(values):
    half = 0.5 * values
    return half + half * jnp.tanh(SLOPE * half)


def twice_slope(halved, bent):
    return (1.0 + bent) * (1.0 + halved * (1.0 - bent))


def body(
    place,
    wide_tile,
    narrow_tile,
    before,
    after,
    conv,
    conv_back,
    conv_back_own,
    mix,
    mix_back,
    gain,
    bias,
    out,
    grads,
    act0,
    act1,
    back1,
    back0,
    mid,
    pre0,
    hid0,
    slope0,
    gsum0,
    hid1,
    gsum1,
    pre1,
    slope1,
    masks,
    sides,
    wide,
    narrow,
):
    rows = out.shape[0]
    tile = out.shape[2]
    bf16, f32 = (jnp.bfloat16, jnp.float32)
    first_row, first_col, total_rows, total_cols = [place[k] for k in range(4)]
    lane = lax.broadcasted_iota(jnp.int32, (CH, LANES), 1)
    column = first_col + jnp.where(lane < LANES - 64, lane, lane - LANES)
    masks[0] = jnp.where((column >= 0) & (column < total_cols), 1.0, 0.0).astype(bf16)
    masks[1] = jnp.where((column > 0) & (column <= total_cols), 1.0, 0.0).astype(bf16)

    side_lane = lax.broadcasted_iota(jnp.int32, (2 * CH, 128), 1)
    wide_slots = 128 // WIDE_COLS
    for base, cols in ((0, WIDE_COLS), (wide_slots, NARROW_COLS)):
        for slot in range(128 // cols):
            here = (side_lane >= slot * cols) & (side_lane < (slot + 1) * cols)
            sides[0, base + slot] = jnp.where(here, 1.0, 0.0).astype(bf16)
            sides[1, base + slot] = jnp.where(here, 0.0, 1.0).astype(bf16)
    own = slice(0, CH)

    def half_in_rows(local_row):
        row = first_row + local_row
        factor = jnp.where((row >= 0) & (row < total_rows), 0.5, 0.0)
        return jnp.broadcast_to(factor, (CH, LANES)).astype(bf16)

    def spread(target, index, values, dilation):
        stores = []
        for step in range(-2, 3):
            moved = values
            if step:
                moved = pltpu.roll(values, (-step * dilation) % LANES, 1)
            stores.append((target, (step + 2, index), moved))
        return stores

    hand_pre, hand_mix = ({}, {})

    def over_rows(count, at_once, *stages):
        def step(m, carry):
            stores = []
            for stage in stages:
                for k in range(at_once):
                    for target, index, values in stage(at_once * m + k, k):
                        if isinstance(target, dict):
                            target[index] = values
                        else:
                            stores.append((target, index, values))
            for target, index, values in stores:
                target[index] = values
            return carry

        lax.fori_loop(0, count // at_once, step, 0)

    def stacked(source, index, dilation, sign, part=slice(None), lanes=slice(None)):
        pieces = []
        for row_shift, col_shift in tap_list(dilation):
            pieces.append(
                source[sign * col_shift // dilation + 2, index + sign * row_shift, part, lanes]
            )
        return jnp.concatenate(pieces, axis=0)

    def dot(left, right):
        return jnp.dot(left, right, preferred_element_type=f32)

    def own_dot(left, right):
        return lax.dot_general(left, right, (((1,), (1,)), ((), ())), preferred_element_type=f32)

    def across(values, count=LANES):
        return jnp.concatenate([values] * (count // 128), axis=1)

    def both_halves(values):
        return jnp.concatenate([values, values], axis=0)

    def with_sides(tile_row, message, slot, cols):
        pick = slot if cols == WIDE_COLS else wide_slots + slot
        both = after[message] * sides[0, pick] + before[message] * sides[1, pick]
        if slot:
            both = pltpu.roll(both, 128 - slot * cols, 1)
        return jnp.concatenate([tile_row, both], axis=1)

    wide_messages = (rows + 2 * WIDE_ROWS) // wide_slots
    narrow_messages = before.shape[0] - wide_messages

    def fill_wide(m, carry):
        stores = []
        for k in range(ACT_ROWS):
            message = m * (ACT_ROWS // wide_slots) + k // wide_slots
            slot = k % wide_slots
            q = message + slot * wide_messages
            row = with_sides(wide_tile[q], message, slot, WIDE_COLS)
            stores.append((wide, q, row))
            stores += spread(act0, q, gated(row.astype(f32)).astype(bf16), FIRST_DILATION)
        for target, index, values in stores:
            target[index] = values
        return carry

    lax.fori_loop(0, (rows + 2 * WIDE_ROWS) // ACT_ROWS, fill_wide, 0)

    def fill_narrow(message, carry):
        for slot in range((rows + 2 * NARROW_ROWS) // narrow_messages):
            n = message + slot * narrow_messages
            narrow[n] = with_sides(
                narrow_tile[n], wide_messages + message, slot, NARROW_COLS
            )
        return carry

    lax.fori_loop(0, narrow_messages, fill_narrow, 0)

    def first_conv(n, k):
        pre = dot(conv[0], stacked(act0, n + FIRST_DILATION, FIRST_DILATION, 1))
        return [(hand_pre, k, pre)]

    def first_mix(n, k):
        pre = hand_pre[k]
        hidden = gated(across(gain[0]) * pre + across(bias[0])).astype(bf16)
        return [
            (hand_mix, k, dot(mix[0], hidden)),
            (pre0, n, pre[:CH]),
            (hid0, n, hidden[:CH, :tile]),
        ]

    def first_mirror(n, k):
        q = n + FIRST_DILATION
        summed = (wide[q].astype(f32) + hand_mix[k]).astype(bf16)
        other = pltpu.roll(summed[CH:], 1, 1)
        both = (summed[:CH] * masks[0] + other * masks[1]) * half_in_rows(q - WIDE_ROWS)
        act = gated(both.astype(f32)).astype(bf16)
        acts = jnp.concatenate([act * masks[0], act * masks[1]], axis=0)
        return spread(act1, n, acts, SECOND_DILATION) + [(mid, n, both)]

    over_rows(
        rows + 2 * (WIDE_ROWS - FIRST_DILATION), FIRST_ROWS, first_conv, first_mix, first_mirror
    )

    def second_conv(n, k):
        pre = dot(conv[1], stacked(act1, n + SECOND_DILATION, SECOND_DILATION, 1))
        cot = narrow[n]
        total = (cot[:CH] + pltpu.roll(cot[CH:], 1, 1)) * jnp.asarray(0.5, bf16)
        sides = jnp.concatenate([total * masks[0], total * masks[1]], axis=0)
        return [
            (hand_pre, k, pre),
            (hand_mix, k, dot(mix_back[1], sides)),
            (gsum1, n, total),
        ]

    def second_slope(n, k):
        pre = hand_pre[k]
        halved = (0.5 * SLOPE) * (across(gain[1]) * pre + across(bias[1]))
        bent = jnp.tanh(halved)
        grad_pre = hand_mix[k] * twice_slope(halved, bent)
        hidden = (halved[:CH, :tile] * (1.0 / SLOPE)) * (1.0 + bent[:CH, :tile])
        grad_conv = (grad_pre * across(gain[1])).astype(bf16)
        return spread(back1, n, grad_conv, SECOND_DILATION) + [
            (pre1, n, pre[:CH, :tile]),
            (slope1, n, grad_pre[:CH, :tile]),
            (hid1, n, hidden.astype(bf16)),
        ]

    over_rows(rows + 2 * NARROW_ROWS, SECOND_ROWS, second_conv, second_slope)

    def between_conv(n, k):
        rows_at = n + SECOND_DILATION
        return [(hand_pre, k, dot(conv_back[...], stacked(back1, rows_at, SECOND_DILATION, -1)))]

    def between_mirror(n, k):
        halved = (0.5 * SLOPE) * mid[n + NARROW_ROWS + FIRST_DILATION].astype(f32)
        slope = twice_slope(halved, jnp.tanh(halved))
        total = gsum1[n + SECOND_DILATION].astype(f32)
        grad_in = (both_halves(total) + both_halves(slope) * hand_pre[k]).astype(bf16)
        both = grad_in[:CH] * masks[0] + grad_in[CH:] * masks[1]
        both = (both * masks[0]) * half_in_rows(n - FIRST_DILATION)
        return [(hand_mix, (k, own), dot(mix_back[0, :CH, :CH], both)), (gsum0, n, both)]

    def between_slope(n, k):
        pre = pre0[n + WIDE_ROWS - 2 * FIRST_DILATION]
        halved = (0.5 * SLOPE) * (across(gain[0, :CH]) * pre + across(bias[0, :CH]))
        grad_pre = hand_mix[k, own] * twice_slope(halved, jnp.tanh(halved))
        grad_conv = (grad_pre * across(gain[0, :CH])).astype(bf16)
        return spread(back0, n, grad_conv, FIRST_DILATION) + [(slope0, n, grad_pre[:, :tile])]

    over_rows(
        rows + 2 * FIRST_DILATION, BETWEEN_ROWS, between_conv, between_mirror, between_slope
    )

    near = slice(0, tile)

    def finish(m, carry):
        conv0, conv1, mix0, mix1, gain0, bias0, gain1, bias1 = carry

        def pair(load):
            return jnp.concatenate([load(2 * m), load(2 * m + 1)], axis=1)

        back = dot(
            conv_back_own[...],
            pair(lambda n: stacked(back0, n + FIRST_DILATION, FIRST_DILATION, -1, own, near)),
        )
        values = pair(lambda n: wide[n + WIDE_ROWS, own, near]).astype(f32)
        halved = (0.5 * SLOPE) * values
        total0 = pair(lambda n: gsum0[n + FIRST_DILATION, :, near])
        result = total0.astype(f32) + twice_slope(halved, jnp.tanh(halved)) * back
        result = result.astype(bf16)
        out[2 * m] = result[:, :tile]
        out[2 * m + 1] = result[:, tile:]
        grad0 = pair(lambda n: back0[2, n + FIRST_DILATION, :, near])
        grad1 = pair(lambda n: back1[2, n + NARROW_ROWS, own, near])
        stack0 = pair(lambda n: stacked(act0, n + WIDE_ROWS, FIRST_DILATION, 1, own, near))
        stack1 = pair(
            lambda n: stacked(
                act1, n + WIDE_ROWS - FIRST_DILATION, SECOND_DILATION, 1, own, near
            )
        )
        conv0 = conv0 + own_dot(grad0, stack0)
        conv1 = conv1 + own_dot(grad1, stack1)
        mix0 = mix0 + own_dot(total0, pair(lambda n: hid0[n + WIDE_ROWS - FIRST_DILATION]))
        total1 = pair(lambda n: gsum1[n + NARROW_ROWS, :, near])
        mix1 = mix1 + own_dot(total1, pair(lambda n: hid1[n + NARROW_ROWS]))
        for n in (2 * m, 2 * m + 1):
            grad = slope0[n + FIRST_DILATION]
            bias0 = bias0 + grad
            gain0 = gain0 + grad * pre0[n + WIDE_ROWS - FIRST_DILATION, :, near]
            grad = slope1[n + NARROW_ROWS]
            bias1 = bias1 + grad
            gain1 = gain1 + grad * pre1[n + NARROW_ROWS]
        return conv0, conv1, mix0, mix1, gain0, bias0, gain1, bias1

    taps_zero = jnp.zeros((CH, TAPS * CH), f32)
    small_zero = jnp.zeros((CH, CH), f32)
    tile_zero = jnp.zeros((CH, tile), f32)
    start = (taps_zero,) * 2 + (small_zero,) * 2 + (tile_zero,) * 4
    conv0, conv1, mix0, mix1, gain0, bias0, gain1, bias1 = lax.fori_loop(
        0, rows // 2, finish, start, unroll=4
    )
    edge = TAPS * CH
    for s, parts in enumerate(((conv0, mix0, gain0, bias0), (conv1, mix1, gain1, bias1))):
        place_s = slice(s * CH, (s + 1) * CH)
        grads[place_s, 0:edge] = parts[0]
        sums = [jnp.sum(part, axis=1, keepdims=True) for part in parts[2:]]
        rest = jnp.zeros((CH, GRAD_COLS - edge - CH - 2), f32)
        grads[place_s, edge:] = jnp.concatenate([parts[1]] + sums + [rest], axis=1)


def swap_mesh_tap(weights):
    return weights.reshape((3, 3) + weights.shape[1:]).swapaxes(0, 1).reshape(weights.shape)


def two_sided(weights):
    other = swap_mesh_tap(weights)
    zero = jnp.zeros_like(weights)
    top = jnp.concatenate([weights, zero], axis=2)
    low = jnp.concatenate([zero, other], axis=2)
    both = jnp.concatenate([top, low], axis=1)
    return both.transpose(1, 0, 2).reshape(2 * CH, TAPS * 2 * CH)


def two_diagonal(weights):
    zero = jnp.zeros_like(weights)
    top = jnp.concatenate([weights, zero], axis=2)
    return jnp.concatenate([top, jnp.concatenate([zero, weights], axis=2)], axis=1)


def on_tile(fields, place, conv_weight, mix_weight, norm_gain, norm_bias, rows, tile):
    bf16, f32 = (jnp.bfloat16, jnp.float32)
    back = 0.5 * conv_weight.swapaxes(2, 3)

    def per_channel(values):
        return jnp.broadcast_to(jnp.tile(values, (1, 2))[:, :, None], (2, 2 * CH, 128))

    operands = (
        place,
        *fields,
        jnp.stack([two_sided(conv_weight[s]) for s in range(2)]),
        two_sided(back[1]),
        back[0].transpose(1, 0, 2).reshape(CH, TAPS * CH),
        two_diagonal(mix_weight),
        two_diagonal(0.5 * mix_weight.swapaxes(1, 2)),
        per_channel(norm_gain),
        per_channel(norm_bias),
    )
    wide_rows = rows + 2 * WIDE_ROWS
    mid_rows = wide_rows - 2 * FIRST_DILATION
    narrow_rows = rows + 2 * NARROW_ROWS
    inner_rows = rows + 2 * FIRST_DILATION
    vmem = pl.BlockSpec(memory_space=pltpu.VMEM)
    return pl.pallas_call(
        body,
        out_shape=(
            jax.ShapeDtypeStruct((rows, CH, tile), bf16),
            jax.ShapeDtypeStruct((2 * CH, GRAD_COLS), f32),
        ),
        in_specs=[pl.BlockSpec(memory_space=pltpu.SMEM)] + [vmem] * (len(operands) - 1),
        out_specs=(vmem, vmem),
        scratch_shapes=[
            pltpu.VMEM((5, wide_rows, 2 * CH, LANES), bf16),
            pltpu.VMEM((5, mid_rows, 2 * CH, LANES), bf16),
            pltpu.VMEM((5, narrow_rows, 2 * CH, LANES), bf16),
            pltpu.VMEM((5, inner_rows, CH, LANES), bf16),
            pltpu.VMEM((mid_rows, CH, LANES), bf16),
            pltpu.VMEM((mid_rows, CH, LANES), f32),
            pltpu.VMEM((mid_rows, CH, tile), bf16),
            pltpu.VMEM((inner_rows, CH, tile), f32),
            pltpu.VMEM((inner_rows, CH, LANES), bf16),
            pltpu.VMEM((narrow_rows, CH, tile), bf16),
            pltpu.VMEM((narrow_rows, CH, LANES), bf16),
            pltpu.VMEM((narrow_rows, CH, tile), f32),
            pltpu.VMEM((narrow_rows, CH, tile), f32),
            pltpu.VMEM((2, CH, LANES), bf16),
            pltpu.VMEM((2, 128 // WIDE_COLS + 128 // NARROW_COLS, 2 * CH, 128), bf16),
            pltpu.VMEM((wide_rows, 2 * CH, LANES), bf16),
            pltpu.VMEM((narrow_rows, 2 * CH, LANES), bf16),
        ],
        compiler_params=pltpu.CompilerParams(vmem_limit_bytes=48 * 1024 * 1024),
        name="blocks_backward",
    )(*operands)


def gather_sides(axis, down, up):
    devices = lax.axis_size(axis)
    odd = lax.axis_index(axis) % 2 == 1
    routes = []
    for start in (0, 1):
        pairs = [(i, i + 1) for i in range(start, devices - 1, 2)]
        routes.append(pairs + [(j, i) for i, j in pairs])
    across = lax.ppermute(jnp.where(odd, down, up), axis, routes[1])
    within = lax.ppermute(jnp.where(odd, up, down), axis, routes[0])
    return jnp.where(odd, within, across), jnp.where(odd, across, within)


def packed(wide, narrow, last):
    def in_slots(rows, cols):
        slots = 128 // cols
        edge = rows[:, :, -cols:] if last else rows[:, :, :cols]
        edge = jnp.concatenate([edge, edge[: -rows.shape[0] % slots]], axis=0)
        pieces = jnp.split(edge, slots, axis=0)
        gap = jnp.zeros(pieces[0].shape[:2] + (128 - slots * cols,), edge.dtype)
        if last:
            return jnp.concatenate(pieces[1:] + [gap] + pieces[:1], axis=2)
        return jnp.concatenate(pieces + [gap], axis=2)

    return jnp.concatenate([in_slots(wide, WIDE_COLS), in_slots(narrow, NARROW_COLS)], axis=0)


def with_surroundings(band, cotangent):
    devices = lax.axis_size("off")
    mine = jnp.concatenate([band, cotangent], axis=1)
    other = lax.ppermute(mine[:, :, ::-1], "off", [(i, devices - 1 - i) for i in range(devices)])
    wide = jnp.concatenate([band, other[:, :CH]], axis=1)
    narrow = jnp.concatenate([cotangent, other[:, CH:]], axis=1)
    before, after = gather_sides(
        "pos",
        jnp.concatenate([wide[-WIDE_ROWS:], narrow[-NARROW_ROWS:]], axis=0),
        jnp.concatenate([wide[:WIDE_ROWS], narrow[:NARROW_ROWS]], axis=0),
    )
    wide = jnp.concatenate([before[:WIDE_ROWS], wide, after[:WIDE_ROWS]], axis=0)
    narrow = jnp.concatenate([before[WIDE_ROWS:], narrow, after[WIDE_ROWS:]], axis=0)
    before, after = gather_sides(
        "off", packed(wide, narrow, True), packed(wide, narrow, False)
    )
    return wide, narrow, before, after


def unpack(scale, blocks, conv, mix, gain, bias, grads):
    edge = TAPS * CH
    count, height = blocks.shape[:2]
    for k in range(count):
        grads[k * height : (k + 1) * height] = blocks[k]
    for s in range(2):
        part = slice(s * CH, (s + 1) * CH)
        for tap in range(TAPS):
            conv[s, tap] = grads[part, tap * CH : (tap + 1) * CH] * scale
        mix[s] = grads[part, edge : edge + CH] * scale
        rest = (grads[part, 2 * 128 : 3 * 128] * scale).T
        start = edge + CH - 2 * 128
        gain[s : s + 1] = rest[start : start + 1]
        bias[s : s + 1] = rest[start + 1 : start + 2]


def unpacked(blocks, scale):
    f32 = jnp.float32
    vmem = pl.BlockSpec(memory_space=pltpu.VMEM)
    return pl.pallas_call(
        functools.partial(unpack, scale),
        out_shape=(
            jax.ShapeDtypeStruct((2, TAPS, CH, CH), f32),
            jax.ShapeDtypeStruct((2, CH, CH), f32),
            jax.ShapeDtypeStruct((2, CH), f32),
            jax.ShapeDtypeStruct((2, CH), f32),
        ),
        in_specs=[vmem],
        out_specs=(vmem,) * 4,
        scratch_shapes=[pltpu.VMEM((2 * CH, GRAD_COLS), f32)],
        name="unpack_gradients",
    )(blocks)


def summed_over_mesh(parts):
    rows, columns = (lax.axis_size("pos"), lax.axis_size("off"))
    size = 2 * columns
    near = [[size * g + i for i in range(size)] for g in range(rows // 2)]
    far = [[2 * g + i for g in range(rows // 2)] for i in range(2)]
    axes = ("pos", "off")

    def exchanged(blocks, axis, groups):
        return lax.all_to_all(blocks, axis, 0, 0, tiled=True, axis_index_groups=groups)

    def copies(part, count):
        return jnp.broadcast_to(part[None], (count,) + part.shape)

    blocks = parts.reshape(size, -1, parts.shape[1])
    part = jnp.sum(exchanged(blocks, axes, near), axis=0)
    part = exchanged(copies(part.astype(jnp.bfloat16), rows // 2), "pos", far)
    part = jnp.sum(part.astype(jnp.float32), axis=0)
    return exchanged(copies(part, size), axes, near)


def local(band_in, conv_weight, mix_weight, norm_gain, norm_bias, cotangent):
    rows, tile = band_in.shape[1:]
    total_rows = rows * lax.axis_size("pos")
    total_cols = tile * lax.axis_size("off")
    grad_scale = 1.0 / math.sqrt(total_rows * total_cols)
    place = jnp.stack(
        [
            lax.axis_index("pos") * rows,
            lax.axis_index("off") * tile,
            jnp.int32(total_rows),
            jnp.int32(total_cols),
        ]
    )
    fields = with_surroundings(band_in.swapaxes(0, 1), cotangent.swapaxes(0, 1))
    gradient, grads = on_tile(
        fields, place, conv_weight, mix_weight, norm_gain, norm_bias, rows, tile
    )
    return (gradient.swapaxes(0, 1), *unpacked(summed_over_mesh(grads), grad_scale))


def solution(mesh):
    placed = (P(None, "pos", "off"), P(), P(), P(), P(), P(None, "pos", "off"))
    return jax.shard_map(
        local,
        mesh=mesh,
        in_specs=placed,
        out_specs=(P(None, "pos", "off"), P(), P(), P(), P()),
        check_vma=False,
    )
```
